32 devices in a mesh: groups: 2 (over y), wide: 4 (over z), narrow: 4 (over x, core).
Axes of the slice: x: 2, y: 2, z: 4, core: 2. Of those that a mesh axis runs over, the one named last changes fastest.
Arguments:
- tokens: bfloat16 [512, 4096], P(('groups', 'wide'), 'narrow'), parts along dimension 0, may hold values from -6 to 6
- routes: int32 [512, 8], P(('groups', 'wide')), parts along dimension 0, may hold values from 0 to 15, all different within a row; in each aligned block of 64 rows (0 to 63, 64 to 127, ...) at most 40 rows name the same one
- gate_weights: float32 [512, 8], P(('groups', 'wide')), parts along dimension 0, may hold values from 0.05 to 1
- delta_of: int32 [16], replicated, may hold values from 0 to 15, each once
- base_gate: bfloat16 [4096, 1536], P('wide', 'narrow'), may hold values from -0.09375 to 0.09375
- base_up: bfloat16 [4096, 1536], P('wide', 'narrow'), may hold values from -0.09375 to 0.09375
- base_down: bfloat16 [1536, 4096], P('wide', 'narrow'), may hold values from -0.15625 to 0.15625
- gate_left: bfloat16 [16, 4096, 32], P('wide', 'narrow'), may hold values from -0.09375 to 0.09375
- gate_right: bfloat16 [16, 32, 1536], P('wide', None, 'narrow'), may hold values from -0.5 to 0.5
- up_left: bfloat16 [16, 4096, 32], P('wide', 'narrow'), may hold values from -0.09375 to 0.09375
- up_right: bfloat16 [16, 32, 1536], P('wide', None, 'narrow'), may hold values from -0.5 to 0.5
- down_left: bfloat16 [16, 1536, 32], P('wide', 'narrow'), may hold values from -0.15625 to 0.15625
- down_right: bfloat16 [16, 32, 4096], P('wide', None, 'narrow'), may hold values from -0.5 to 0.5
Outputs:
- mixed_out: bfloat16 [512, 4096], P(('groups', 'wide'), 'narrow'), parts along dimension 0
The draws below stay inside these ranges and needn't reach their ends.
There are 2 independent parts, one for each index of `groups`. The reference program is written for one: setup_inputs(seed, part) draws one part's arguments, and reference() takes and returns one part's arrays. A program takes and returns all parts, laid end to end along the dimension named above; an argument that names none is the same for every part. Nothing has to cross between parts.
Inputs may be any that keep to these rules, and one draw needn't show every extreme that they name: `routes`: in each aligned block of 64 rows (the rows of one index of wide) no expert is named by more than 40 rows, and in some block some expert is named by exactly 40 rows.
All inputs are finite; a program needn't handle non-finite values.
Results may differ from the reference program's by a relative error of at most 0.0053.
Values may be sent and summed in bfloat16 or wider, within the bound.
A program may use at most 64 MiB of HBM per device.

```python
import math
import jax
import jax.numpy as jnp
import numpy as np
from jax import lax

D = 4096
FF = 1536
R = 32
TOP = 8
BLK = 64
EXPERTS = 16
TOKENS = 256
CAP = 40


def steps_of(rng, extent, shards, least, high):
    gain, own = 1.0, jax.random.fold_in(rng, 6)
    for position, shards_of in shards:
        heights = jnp.exp(jax.random.uniform(jax.random.fold_in(own, position), (shards_of,), jnp.float32, least / len(shards), high / len(shards)))
        gain = gain * jnp.repeat(heights, extent[position] // shards_of).reshape([-1 if axis == position else 1 for axis in range(len(extent))])
    return gain


def deal_out(own_key, own, number, rows, count, top, bound, lean):
    order = jax.random.permutation(own_key, count)
    crowded, common = portions_of(count, rows * top, bound, lean, True), portions_of(count, rows * top, bound, lean, False)
    places = jnp.arange(count)

    def named(lengths, rotation):
        used = int((lengths > 0).sum())
        fixed = max(1, used // 4)
        moved = fixed + (places - fixed + rotation * (used - fixed)) % max(1, count - fixed)
        return jnp.zeros((count,), jnp.int32).at[order[jnp.where(places < fixed, places, moved)]].set(jnp.asarray(lengths, jnp.int32))

    lengths = jnp.where(number % 4 == 0, named(crowded, number // 4), named(common, number - number // 4 - 1))
    mixed = jax.random.permutation(jax.random.fold_in(own, 3), count)
    giver, sink = mixed[0:count // 2 * 2:2], mixed[1:count // 2 * 2:2]
    slack = jnp.minimum(lengths[giver] - 1, bound - lengths[sink]) // 2
    slack = jnp.where((giver == order[0]) | (sink == order[0]) | (lengths[sink] == 0), 0, jnp.maximum(slack, 0))
    moved = jax.random.randint(jax.random.fold_in(own, 4), (count // 2,), 0, 1 << 20) % (slack + 1)
    lengths = lengths.at[giver].add(-moved).at[sink].add(moved)
    items = jnp.searchsorted(jnp.cumsum(lengths), jnp.arange(rows * top), side="right").astype(jnp.int32)
    table = items.reshape(top, rows).T
    table = table[jax.random.permutation(jax.random.fold_in(own, 1), rows)]
    rotation = jax.random.randint(jax.random.fold_in(own, 2), (rows, 1), 0, top)
    return jnp.take_along_axis(table, (jnp.arange(top)[None, :] + rotation) % top, axis=1)


def portions_of(count, total, most, lean, full):
    portions = [(1 << 20) // math.isqrt(rank ** lean) + 1 for rank in range(1, count + 1)]
    largest = most if full else min(most, max(-(-total // count), total * portions[0] // sum(portions)))
    least = 1 if total - largest >= count - 1 else 0
    given, surplus = [largest] + [least] * (count - 1), total - largest - least * (count - 1)
    while surplus > 0:
        free = [i for i in range(1, count) if given[i] < largest] or [i for i in range(1, count) if given[i] < most]
        whole, remaining = sum([portions[i] for i in free]), surplus
        for i in free:
            more = min(most - given[i], max(1, remaining * portions[i] // whole), surplus)
            given[i] = given[i] + more
            surplus = surplus - more
    return np.array(given)


def gaussian(rng, dims, width, bound, split=(), kind=jnp.bfloat16):
    array = width * jax.random.normal(rng, dims, jnp.float32)
    if split:
        array = array * steps_of(rng, dims, split, -0.22, 0.18)
    return jnp.clip(array, -bound, bound).astype(kind)


def setup_inputs(seed: int = 0, part: int = 0) -> dict:
    arg_keys = jax.random.split(jax.random.key(seed), 14)
    part_splits = jax.random.split(jax.random.fold_in(arg_keys[13], part), 14)
    tokens = gaussian(part_splits[0], (TOKENS, D), 1.0, 6.0, ((0, 4), (1, 4)))
    routes_keys = jax.random.split(jax.random.fold_in(part_splits[1], 1), TOKENS // BLK)
    routes_turns = jax.random.permutation(jax.random.fold_in(part_splits[1], 3), TOKENS // BLK)
    routes = jax.vmap(lambda own, number: deal_out(jax.random.fold_in(part_splits[1], 2), own, number, BLK, EXPERTS, TOP, CAP, 2))(routes_keys, routes_turns).reshape((TOKENS, TOP))
    gate_weights = jnp.clip(0.05 + 0.95 * jax.random.uniform(part_splits[2], (TOKENS, TOP), jnp.float32) ** steps_of(part_splits[2], (TOKENS, TOP), ((0, 4),), -0.2, 0.2), 0.05, 1.0)
    delta_of = jax.random.permutation(arg_keys[3], EXPERTS).astype(jnp.int32)
    base_gate = gaussian(arg_keys[4], (D, FF), D ** -0.5, 0.09375, ((0, 4), (1, 4)))
    base_up = gaussian(arg_keys[5], (D, FF), D ** -0.5, 0.09375, ((0, 4), (1, 4)))
    base_down = gaussian(arg_keys[6], (FF, D), FF ** -0.5, 0.15625, ((0, 4), (1, 4)))
    gate_left = gaussian(arg_keys[7], (EXPERTS, D, R), D ** -0.5, 0.09375, ((0, 4), (1, 4)))
    gate_right = gaussian(arg_keys[8], (EXPERTS, R, FF), (4 * R) ** -0.5, 0.5, ((0, 4), (2, 4)))
    up_left = gaussian(arg_keys[9], (EXPERTS, D, R), D ** -0.5, 0.09375, ((0, 4), (1, 4)))
    up_right = gaussian(arg_keys[10], (EXPERTS, R, FF), (4 * R) ** -0.5, 0.5, ((0, 4), (2, 4)))
    down_left = gaussian(arg_keys[11], (EXPERTS, FF, R), FF ** -0.5, 0.15625, ((0, 4), (1, 4)))
    down_right = gaussian(arg_keys[12], (EXPERTS, R, D), (4 * R) ** -0.5, 0.5, ((0, 4), (2, 4)))
    return {"tokens": tokens, "routes": routes, "gate_weights": gate_weights, "delta_of": delta_of, "base_gate": base_gate, "base_up": base_up, "base_down": base_down, "gate_left": gate_left, "gate_right": gate_right, "up_left": up_left, "up_right": up_right, "down_left": down_left, "down_right": down_right}


def rebuild(base, left, right):
    return (base.astype(jnp.float32) + jnp.dot(left, right, preferred_element_type=jnp.float32)).astype(jnp.bfloat16)


def reference(tokens, routes, gate_weights, delta_of, base_gate, base_up, base_down, gate_left, gate_right, up_left, up_right, down_left, down_right):
    token_count = tokens.shape[0]
    experts = delta_of.shape[0]
    expert_ids = jnp.arange(experts, dtype=jnp.int32)
    onehot = (routes[:, :, None] == expert_ids[None, None, :]).astype(jnp.int32)
    routed = jnp.sum(onehot, axis=1)
    blocked = routed.reshape(token_count // BLK, BLK, experts)
    before = (jnp.cumsum(blocked, axis=1) - blocked).reshape(token_count, experts)
    place_in = jnp.sum(onehot * before[:, None, :], axis=2).astype(jnp.int32)
    block_of = (jnp.arange(token_count, dtype=jnp.int32) // BLK)[:, None]
    slot_count = (token_count // BLK) * CAP
    flat_index = (routes * slot_count + block_of * CAP + place_in).reshape(-1).astype(jnp.int32)
    token_ids = jnp.repeat(jnp.arange(token_count, dtype=jnp.int32), routes.shape[1])
    source = jnp.full((experts * slot_count,), token_count, jnp.int32).at[flat_index].set(token_ids).reshape(experts, slot_count)
    scales = jnp.zeros((experts * slot_count,), jnp.float32).at[flat_index].set(gate_weights.reshape(-1).astype(jnp.float32)).reshape(experts, slot_count)
    padded = jnp.concatenate([tokens, jnp.zeros((1, tokens.shape[1]), tokens.dtype)], axis=0)

    def visit(running, inputs):
        expert, row_ids, row_scales = inputs
        delta_id = delta_of[expert]
        w_gate = rebuild(base_gate, gate_left[delta_id], gate_right[delta_id])
        w_up = rebuild(base_up, up_left[delta_id], up_right[delta_id])
        w_down = rebuild(base_down, down_left[delta_id], down_right[delta_id])
        rows_in = padded[row_ids]
        gate_act = jnp.dot(rows_in, w_gate, preferred_element_type=jnp.float32)
        up_act = jnp.dot(rows_in, w_up, preferred_element_type=jnp.float32)
        hidden = (jax.nn.silu(gate_act) * up_act).astype(jnp.bfloat16)
        result = jnp.dot(hidden, w_down, preferred_element_type=jnp.float32).astype(jnp.bfloat16)
        running = running.at[row_ids].add(row_scales[:, None] * result.astype(jnp.float32))
        return running, None

    start_sum = jnp.zeros((token_count + 1, tokens.shape[1]), jnp.float32)
    running, unused = lax.scan(visit, start_sum, (expert_ids, source, scales))
    return running[:token_count].astype(jnp.bfloat16)
```

```python
import jax
import jax.numpy as jnp
from jax import lax
from jax.sharding import PartitionSpec as P


def dot32(a, b):
    return jnp.dot(a, b, preferred_element_type=jnp.float32)


def shards(
    tokens,
    routes,
    gate_weights,
    delta_of,
    base_gate,
    base_up,
    base_down,
    gate_left,
    gate_right,
    up_left,
    up_right,
    down_left,
    down_right,
):
    exp_here, _, rank = gate_left.shape
    experts = delta_of.shape[0]
    mine = lax.axis_index("wide")
    bf16 = jnp.bfloat16

    expert_ids = lax.broadcasted_iota(jnp.int32, (1, 1, experts), 2)
    named = routes[:, :, None] == expert_ids
    delta_ids = jnp.sum(jnp.where(named, delta_of[None, None, :], 0), axis=2)
    weight_of = jnp.sum(
        jnp.where(delta_ids[:, :, None] == expert_ids, gate_weights[:, :, None], 0.0), axis=1
    )
    weights = lax.all_gather(weight_of, "wide", axis=0, tiled=True)
    weights = lax.dynamic_slice_in_dim(weights, mine * exp_here, exp_here, axis=1)

    rows = lax.all_gather(tokens, "wide", axis=0, tiled=True)
    full = lax.all_gather(rows, "narrow", axis=1, tiled=True)
    depth = base_gate.shape[0]
    part = lax.dynamic_slice_in_dim(full, mine * depth, depth, axis=1)

    base_both = jnp.concatenate([base_gate, base_up], axis=1)
    both = lax.psum(dot32(part, base_both), "wide")
    columns = base_gate.shape[1]

    lefts = jnp.concatenate([gate_left, up_left], axis=0)
    low = lax.psum(jnp.einsum("td,edr->ter", rows, lefts, preferred_element_type=jnp.float32), "narrow")
    low = low.astype(bf16)

    mixed = 0.0
    thin = []
    for e in range(exp_here):
        gate = both[:, :columns] + dot32(low[:, e], gate_right[e])
        up = both[:, columns:] + dot32(low[:, exp_here + e], up_right[e])
        hidden = jax.nn.silu(gate) * up * weights[:, e : e + 1]
        mixed = mixed + hidden
        thin.append(dot32(hidden.astype(bf16), down_left[e]))
    mixed = lax.psum(mixed, "wide").astype(bf16)
    mixed_full = lax.all_gather(mixed, "narrow", axis=1, tiled=True)
    depth = base_down.shape[0]
    mixed_part = lax.dynamic_slice_in_dim(mixed_full, mine * depth, depth, axis=1)
    thin = lax.psum(jnp.concatenate(thin, axis=1), "narrow").astype(bf16)
    out = dot32(mixed_part, base_down) + dot32(thin, down_right.reshape(exp_here * rank, -1))
    out = lax.psum_scatter(out, "wide", scatter_dimension=0, tiled=True)
    return out.astype(bf16)


def solution(mesh):
    return jax.shard_map(
        shards,
        mesh=mesh,
        in_specs=(
            P(("groups", "wide"), "narrow"),
            P(("groups", "wide"), None),
            P(("groups", "wide"), None),
            P(),
            P("wide", "narrow"),
            P("wide", "narrow"),
            P("wide", "narrow"),
            P("wide", "narrow", None),
            P("wide", None, "narrow"),
            P("wide", "narrow", None),
            P("wide", None, "narrow"),
            P("wide", "narrow", None),
            P("wide", None, "narrow"),
        ),
        out_specs=P(("groups", "wide"), "narrow"),
        check_vma=False,
    )
```

```python
import jax
import jax.numpy as jnp
from jax import lax
from jax.experimental import pallas as pl
from jax.experimental.pallas import tpu as pltpu
from jax.sharding import PartitionSpec as P


def dot32(a, b):
    return jnp.dot(a, b, preferred_element_type=jnp.float32)


PLANE = 4


def kernel(
    tok, wt, bg, bu, bd, gl, gr, ul, ur, dl, dr, out,
    xcol, xw, wts, gsend, grecv, gown, gred, gall, apart, asend, arecv, afin,
    hacc, hsend, hrecv, hpl, bpart, bsend, brecv, bfin, osend, orecv, oown,
    tok_s, tok_r, wt_s, wt_r, bs_s, bs_r, g_s, g_r, ga_s, ga_r, a_s, a_r,
    h_s, h_r, hb_s, hb_r, b_s, b_r, o_s, o_r,
):
    bf16, f32 = jnp.bfloat16, jnp.float32
    count = PLANE
    w, n = lax.axis_index("wide"), lax.axis_index("narrow")
    exp_here, rank = gl.shape[0], gl.shape[2]
    cols = bg.shape[1]
    span = exp_here * rank
    pair = n + 1 - 2 * lax.rem(n, 2)
    across = lax.rem(n + 2, count)
    root = n == w
    relay = n == lax.rem(w + 2, count)

    def up_of(d):
        return lax.rem(w + d, count)

    def copy(src, dst, ss, rs, axis, peer):
        return pltpu.make_async_remote_copy(
            src_ref=src, dst_ref=dst, send_sem=ss, recv_sem=rs,
            device_id={axis: peer}, device_id_type=pl.DeviceIdType.MESH,
        )

    barrier = pltpu.get_barrier_semaphore()
    for d in range(1, count):
        pl.semaphore_signal(barrier, inc=1, device_id={"wide": up_of(d)}, device_id_type=pl.DeviceIdType.MESH)
    for peer in (pair, across):
        pl.semaphore_signal(barrier, inc=1, device_id={"narrow": peer}, device_id_type=pl.DeviceIdType.MESH)
    pl.semaphore_wait(barrier, count + 1)

    def tok_copy(d):
        return copy(tok, xcol.at[w], tok_s.at[d], tok_r.at[d], "wide", up_of(d))

    def wt_copy(d):
        return copy(wt, wts.at[w], wt_s.at[d], wt_r.at[d], "wide", up_of(d))

    def pair_copy(d, src):
        return copy(src, xw.at[up_of(count - d)], bs_s.at[d, 0], bs_r.at[d], "narrow", pair)

    def across_copy(d, src):
        return copy(src, xw.at[up_of(count - d)], bs_s.at[d, 1], bs_r.at[d], "narrow", across)

    for d in range(1, count):
        tok_copy(d).start()

    def low(rows, b):
        for e in range(exp_here):
            apart[b, :, e * rank : (e + 1) * rank] = dot32(rows, gl[e])
            apart[b, :, span + e * rank : span + (e + 1) * rank] = dot32(rows, ul[e])

    for d in range(count):
        b = up_of(count - d)
        if d > 0:
            tok_copy(d).wait_recv()
        mine = tok if d == 0 else xcol.at[b]

        @pl.when(root)
        def _():
            across_copy(d, mine).start()
            pair_copy(d, mine).start()
            xw[b] = mine[...]

        low(mine[...], b)

        @pl.when(jnp.logical_not(root))
        def _():
            pair_copy(d, xw.at[b]).wait_recv()

        @pl.when(relay)
        def _():
            pair_copy(d, xw.at[b]).start()

        rows = xw[b]
        gate, up = dot32(rows, bg[...]), dot32(rows, bu[...])
        if d == 0:
            gown[:, :cols] = gate
            gown[:, cols:] = up
            for k in range(1, count):
                wt_copy(k).start()
        else:
            gsend[b, :, :cols] = gate.astype(bf16)
            gsend[b, :, cols:] = up.astype(bf16)
            copy(gsend.at[b], grecv.at[w], g_s.at[d], g_r.at[d], "wide", b).start()

    def a_copy(k):
        return copy(asend.at[k], arecv.at[k], a_s.at[k], a_r.at[k], "narrow", (pair, across)[k])

    asend[0] = apart[...].astype(bf16)
    a_copy(0).start()
    a_copy(0).wait_recv()
    apart[...] = apart[...] + arecv[0].astype(f32)
    asend[1] = apart[...].astype(bf16)
    a_copy(1).start()

    def ga_copy(d):
        return copy(gred, gall.at[w], ga_s.at[d], ga_r.at[d], "wide", up_of(d))

    total = gown[...]
    for d in range(1, count):
        s = up_of(d)
        copy(gsend.at[s], grecv.at[s], g_s.at[d], g_r.at[d], "wide", s).wait_recv()
        total = total + grecv[s].astype(f32)
    gown[...] = total
    gred[...] = total.astype(bf16)
    for d in range(1, count):
        ga_copy(d).start()

    a_copy(1).wait_recv()
    afin[...] = (apart[...] + arecv[1].astype(f32)).astype(bf16)

    for d in range(count):
        b = up_of(count - d)
        if d > 0:
            ga_copy(d).wait_recv()
            wt_copy(d).wait_recv()
            gates, ups = gall[b, :, :cols].astype(f32), gall[b, :, cols:].astype(f32)
            scales = wts[b]
        else:
            gates, ups = gown[:, :cols], gown[:, cols:]
            scales = wt[...]
        ids = lax.broadcasted_iota(jnp.int32, scales.shape, 1)
        thin_rows = afin[b]
        acc = None
        for e in range(exp_here):
            scale = jnp.sum(jnp.where(ids == w * exp_here + e, scales, 0.0), axis=1, keepdims=True)
            gate = gates + dot32(thin_rows[:, e * rank : (e + 1) * rank], gr[e])
            up = ups + dot32(thin_rows[:, span + e * rank : span + (e + 1) * rank], ur[e])
            hidden = gate / (1.0 + jnp.exp(-gate)) * up * scale
            acc = hidden if acc is None else acc + hidden
            bpart[b, :, e * rank : (e + 1) * rank] = dot32(hidden.astype(bf16), dl[e])
        hacc[b] = acc
        hsend[b] = acc.astype(bf16)

    def h_copy(slot, target):
        return copy(hsend, hrecv.at[slot], h_s, h_r.at[slot], "wide", target)

    @pl.when(jnp.logical_not(root))
    def _():
        h_copy(w, n).start()

    def b_copy(k):
        return copy(bsend.at[k], brecv.at[k], b_s.at[k], b_r.at[k], "narrow", (pair, across)[k])

    bsend[0] = bpart[...].astype(bf16)
    b_copy(0).start()
    b_copy(0).wait_recv()
    bpart[...] = bpart[...] + brecv[0].astype(f32)
    bsend[1] = bpart[...].astype(bf16)
    b_copy(1).start()
    b_copy(1).wait_recv()
    bfin[...] = (bpart[...] + brecv[1].astype(f32)).astype(bf16)

    def hpair():
        return copy(hpl, hpl, hb_s.at[0], hb_r, "narrow", pair)

    def hacross():
        return copy(hpl, hpl, hb_s.at[1], hb_r, "narrow", across)

    @pl.when(root)
    def _():
        whole = hacc[...]
        for d in range(1, count):
            s = up_of(d)
            h_copy(s, s).wait_recv()
            whole = whole + hrecv[s].astype(f32)
        hpl[...] = whole.astype(bf16)
        hacross().start()
        hpair().start()

    @pl.when(jnp.logical_not(root))
    def _():
        hpair().wait_recv()

    @pl.when(relay)
    def _():
        hpair().start()

    for d in (2, 1, 3, 0):
        b = up_of(count - d)
        part = dot32(hpl[b], bd[...]) + dot32(bfin[b], dr[...])
        if d == 0:
            oown[...] = part
        else:
            osend[b] = part.astype(bf16)
            copy(osend.at[b], orecv.at[w], o_s.at[d], o_r.at[d], "wide", b).start()
    total = oown[...]
    for d in (1, 3, 2):
        s = up_of(d)
        copy(osend.at[s], orecv.at[s], o_s.at[d], o_r.at[d], "wide", s).wait_recv()
        total = total + orecv[s].astype(f32)
    out[...] = total.astype(bf16)

    for d in range(1, count):
        b = up_of(count - d)
        tok_copy(d).wait_send()
        wt_copy(d).wait_send()
        ga_copy(d).wait_send()
        copy(gsend.at[b], grecv.at[w], g_s.at[d], g_r.at[d], "wide", b).wait_send()
        copy(osend.at[b], orecv.at[w], o_s.at[d], o_r.at[d], "wide", b).wait_send()
    for k in range(2):
        a_copy(k).wait_send()
        b_copy(k).wait_send()

    @pl.when(root)
    def _():
        for d in range(count):
            src = tok if d == 0 else xcol.at[up_of(count - d)]
            across_copy(d, src).wait_send()
            pair_copy(d, src).wait_send()
        hacross().wait_send()
        hpair().wait_send()

    @pl.when(relay)
    def _():
        for d in range(count):
            pair_copy(d, xw.at[up_of(count - d)]).wait_send()
        hpair().wait_send()

    @pl.when(jnp.logical_not(root))
    def _():
        h_copy(w, n).wait_send()


def fused(tokens, weight_of, bg, bu, bd, gl, gr, ul, ur, dl, dr):
    bf16, f32 = jnp.bfloat16, jnp.float32
    count = PLANE
    rows, feats = tokens.shape
    cols = bg.shape[1]
    exp_here, rank = gl.shape[0], gl.shape[2]
    span = exp_here * rank
    lanes = -(-weight_of.shape[1] // 128) * 128
    wt = jnp.pad(weight_of, ((0, 0), (0, lanes - weight_of.shape[1])))
    sem = pltpu.SemaphoreType.DMA
    vm = pltpu.VMEM
    out_feats = bd.shape[1]
    return pl.pallas_call(
        kernel,
        out_shape=jax.ShapeDtypeStruct((rows, out_feats), bf16),
        in_specs=[pl.BlockSpec(memory_space=pltpu.VMEM)] * 11,
        out_specs=pl.BlockSpec(memory_space=pltpu.VMEM),
        scratch_shapes=[
            vm((count, rows, feats), bf16),
            vm((count, rows, feats), bf16),
            vm((count, rows, lanes), f32),
            vm((count, rows, 2 * cols), bf16),
            vm((count, rows, 2 * cols), bf16),
            vm((rows, 2 * cols), f32),
            vm((rows, 2 * cols), bf16),
            vm((count, rows, 2 * cols), bf16),
            vm((count, rows, 2 * span), f32),
            vm((2, count, rows, 2 * span), bf16),
            vm((2, count, rows, 2 * span), bf16),
            vm((count, rows, 2 * span), bf16),
            vm((count, rows, cols), f32),
            vm((count, rows, cols), bf16),
            vm((count, count, rows, cols), bf16),
            vm((count, rows, cols), bf16),
            vm((count, rows, span), f32),
            vm((2, count, rows, span), bf16),
            vm((2, count, rows, span), bf16),
            vm((count, rows, span), bf16),
            vm((count, rows, out_feats), bf16),
            vm((count, rows, out_feats), bf16),
            vm((rows, out_feats), f32),
            sem((count,)), sem((count,)), sem((count,)), sem((count,)),
            sem((count, 2)), sem((count,)),
            sem((count,)), sem((count,)), sem((count,)), sem((count,)),
            sem((2,)), sem((2,)),
            sem, sem((count,)), sem((2,)), sem,
            sem((2,)), sem((2,)), sem((count,)), sem((count,)),
        ],
        compiler_params=pltpu.CompilerParams(collective_id=0, has_side_effects=True, vmem_limit_bytes=60 * 1024 * 1024),
    )(tokens, wt, bg, bu, bd, gl, gr, ul, ur, dl, dr.reshape(span, out_feats))


def shards(
    tokens,
    routes,
    gate_weights,
    delta_of,
    base_gate,
    base_up,
    base_down,
    gate_left,
    gate_right,
    up_left,
    up_right,
    down_left,
    down_right,
):
    exp_here, _, rank = gate_left.shape
    experts = delta_of.shape[0]
    mine = lax.axis_index("wide")
    bf16 = jnp.bfloat16

    expert_ids = lax.broadcasted_iota(jnp.int32, (1, 1, experts), 2)
    named = routes[:, :, None] == expert_ids
    delta_ids = jnp.sum(jnp.where(named, delta_of[None, None, :], 0), axis=2)
    weight_of = jnp.sum(
        jnp.where(delta_ids[:, :, None] == expert_ids, gate_weights[:, :, None], 0.0), axis=1
    )
    if lax.axis_size("narrow") == PLANE and lax.axis_size("wide") == PLANE:
        return fused(tokens, weight_of, base_gate, base_up, base_down, gate_left, gate_right, up_left, up_right, down_left, down_right)
    weights = lax.all_gather(weight_of, "wide", axis=0, tiled=True)
    weights = lax.dynamic_slice_in_dim(weights, mine * exp_here, exp_here, axis=1)

    rows = lax.all_gather(tokens, "wide", axis=0, tiled=True)
    full = lax.all_gather(rows, "narrow", axis=1, tiled=True)
    depth = base_gate.shape[0]
    part = lax.dynamic_slice_in_dim(full, mine * depth, depth, axis=1)

    base_both = jnp.concatenate([base_gate, base_up], axis=1)
    both = lax.psum(dot32(part, base_both), "wide")
    columns = base_gate.shape[1]

    lefts = jnp.concatenate([gate_left, up_left], axis=0)
    low = lax.psum(jnp.einsum("td,edr->ter", rows, lefts, preferred_element_type=jnp.float32), "narrow")
    low = low.astype(bf16)

    mixed = 0.0
    thin = []
    for e in range(exp_here):
        gate = both[:, :columns] + dot32(low[:, e], gate_right[e])
        up = both[:, columns:] + dot32(low[:, exp_here + e], up_right[e])
        hidden = jax.nn.silu(gate) * up * weights[:, e : e + 1]
        mixed = mixed + hidden
        thin.append(dot32(hidden.astype(bf16), down_left[e]))
    mixed = lax.psum(mixed, "wide").astype(bf16)
    mixed_full = lax.all_gather(mixed, "narrow", axis=1, tiled=True)
    depth = base_down.shape[0]
    mixed_part = lax.dynamic_slice_in_dim(mixed_full, mine * depth, depth, axis=1)
    thin = lax.psum(jnp.concatenate(thin, axis=1), "narrow").astype(bf16)
    out = dot32(mixed_part, base_down) + dot32(thin, down_right.reshape(exp_here * rank, -1))
    out = lax.psum_scatter(out, "wide", scatter_dimension=0, tiled=True)
    return out.astype(bf16)


def solution(mesh):
    return jax.shard_map(
        shards,
        mesh=mesh,
        in_specs=(
            P(("groups", "wide"), "narrow"),
            P(("groups", "wide"), None),
            P(("groups", "wide"), None),
            P(),
            P("wide", "narrow"),
            P("wide", "narrow"),
            P("wide", "narrow"),
            P("wide", "narrow", None),
            P("wide", None, "narrow"),
            P("wide", "narrow", None),
            P("wide", None, "narrow"),
            P("wide", "narrow", None),
            P("wide", None, "narrow"),
        ),
        out_specs=P(("groups", "wide"), "narrow"),
        check_vma=False,
    )
```

```python
import jax
import jax.numpy as jnp
from jax import lax
from jax.experimental import pallas as pl
from jax.experimental.pallas import tpu as pltpu
from jax.sharding import PartitionSpec as P


def dot32(a, b):
    return jnp.dot(a, b, preferred_element_type=jnp.float32)


def dot32t(a, b):
    return lax.dot_general(a, b, (((1,), (1,)), ((), ())), preferred_element_type=jnp.float32)


PLANE = 4


def kernel(
    tok, routes, shares, delta, bg_hbm, bu_hbm, bd_hbm, gl_hbm, gr, ul_hbm, ur, dl, dr_hbm, out,
    wt, bgu, lefts, bd, dr,
    xcol, xw, wts, gsend, grecv, gown, gred, gall, apart, asend, arecv, afin,
    hacc, hsend, hrecv, hpl, bpart, bsend, brecv, bfin, osend, orecv, oown,
    tok_s, tok_r, wt_s, wt_r, bs_s, bs_r, g_s, g_r, ga_s, ga_r, a_s, a_r,
    h_s, h_r, hb_s, hb_r, b_s, b_r, o_s, o_r, in_s,
):
    bf16, f32 = jnp.bfloat16, jnp.float32
    count = PLANE
    w, n = lax.axis_index("wide"), lax.axis_index("narrow")
    exp_here, rank, cols = gr.shape
    span = exp_here * rank
    loads = [
        pltpu.make_async_copy(gl_hbm, lefts.at[pl.ds(0, span)], in_s.at[0]),
        pltpu.make_async_copy(ul_hbm, lefts.at[pl.ds(span, span)], in_s.at[1]),
        pltpu.make_async_copy(bg_hbm, bgu.at[:, pl.ds(0, cols)], in_s.at[2]),
        pltpu.make_async_copy(bu_hbm, bgu.at[:, pl.ds(cols, cols)], in_s.at[3]),
        pltpu.make_async_copy(bd_hbm, bd, in_s.at[4]),
        pltpu.make_async_copy(dr_hbm, dr, in_s.at[5]),
    ]
    for load in loads:
        load.start()
    pair = n + 1 - 2 * lax.rem(n, 2)
    across = lax.rem(n + 2, count)
    root = n == w
    relay = n == lax.rem(w + 2, count)

    def up_of(d):
        return lax.rem(w + d, count)

    def copy(src, dst, ss, rs, axis, peer):
        return pltpu.make_async_remote_copy(
            src_ref=src, dst_ref=dst, send_sem=ss, recv_sem=rs,
            device_id={axis: peer}, device_id_type=pl.DeviceIdType.MESH,
        )

    barrier = pltpu.get_barrier_semaphore()
    for d in range(1, count):
        pl.semaphore_signal(barrier, inc=1, device_id={"wide": up_of(d)}, device_id_type=pl.DeviceIdType.MESH)
    for peer in (pair, across):
        pl.semaphore_signal(barrier, inc=1, device_id={"narrow": peer}, device_id_type=pl.DeviceIdType.MESH)
    pl.semaphore_wait(barrier, count + 1)

    def tok_copy(d):
        return copy(tok, xcol.at[w], tok_s.at[d], tok_r.at[d], "wide", up_of(d))

    def wt_copy(d):
        return copy(wt, wts.at[w], wt_s.at[d], wt_r.at[d], "wide", up_of(d))

    def pair_copy(d, src):
        return copy(src, xw.at[up_of(count - d)], bs_s.at[d, 0], bs_r.at[d], "narrow", pair)

    def across_copy(d, src):
        return copy(src, xw.at[up_of(count - d)], bs_s.at[d, 1], bs_r.at[d], "narrow", across)

    for d in range(1, count):
        tok_copy(d).start()

    named, ids = routes[...], jnp.zeros(routes.shape, jnp.int32)
    for e in range(delta.shape[0]):
        ids = jnp.where(named == e, delta[e], ids)
    lanes = lax.broadcasted_iota(jnp.int32, wt.shape, 1)
    table = jnp.zeros(wt.shape, f32)
    for k in range(routes.shape[1]):
        table = table + jnp.where(lanes == ids[:, k : k + 1], shares[:, k : k + 1], 0.0)
    wt[...] = table
    for load in loads[:4]:
        load.wait()

    def low(rows, b):
        apart[b] = dot32t(rows, lefts[...])

    for d in range(count):
        b = up_of(count - d)
        if d > 0:
            tok_copy(d).wait_recv()
        mine = tok if d == 0 else xcol.at[b]

        @pl.when(root)
        def _():
            across_copy(d, mine).start()
            pair_copy(d, mine).start()
            xw[b] = mine[...]

        low(mine[...], b)

        @pl.when(jnp.logical_not(root))
        def _():
            pair_copy(d, xw.at[b]).wait_recv()

        @pl.when(relay)
        def _():
            pair_copy(d, xw.at[b]).start()

        rows = xw[b]
        both = dot32(rows, bgu[...])
        if d == 0:
            gown[...] = both
            for k in range(1, count):
                wt_copy(k).start()
        else:
            gsend[b] = both.astype(bf16)
            copy(gsend.at[b], grecv.at[w], g_s.at[d], g_r.at[d], "wide", b).start()

    def a_copy(k):
        return copy(asend.at[k], arecv.at[k], a_s.at[k], a_r.at[k], "narrow", (pair, across)[k])

    asend[0] = apart[...].astype(bf16)
    a_copy(0).start()
    a_copy(0).wait_recv()
    apart[...] = apart[...] + arecv[0].astype(f32)
    asend[1] = apart[...].astype(bf16)
    a_copy(1).start()

    def ga_copy(d):
        return copy(gred, gall.at[w], ga_s.at[d], ga_r.at[d], "wide", up_of(d))

    total = gown[...]
    for d in range(1, count):
        s = up_of(d)
        copy(gsend.at[s], grecv.at[s], g_s.at[d], g_r.at[d], "wide", s).wait_recv()
        total = total + grecv[s].astype(f32)
    gown[...] = total
    gred[...] = total.astype(bf16)
    for d in range(1, count):
        ga_copy(d).start()

    a_copy(1).wait_recv()
    afin[...] = (apart[...] + arecv[1].astype(f32)).astype(bf16)

    def h_copy(slot, block, d, target):
        return copy(hsend.at[block], hrecv.at[slot, block], h_s.at[d], h_r.at[slot, block], "wide", target)

    for d in range(count):
        b = up_of(count - d)
        if d > 0:
            ga_copy(d).wait_recv()
            wt_copy(d).wait_recv()
            gates, ups = gall[b, :, :cols].astype(f32), gall[b, :, cols:].astype(f32)
            scales = wts[b]
        else:
            gates, ups = gown[:, :cols], gown[:, cols:]
            scales = wt[...]
        ids = lax.broadcasted_iota(jnp.int32, scales.shape, 1)
        thin_rows = afin[b]
        acc = None
        for e in range(exp_here):
            scale = jnp.sum(jnp.where(ids == w * exp_here + e, scales, 0.0), axis=1, keepdims=True)
            gate = gates + dot32(thin_rows[:, e * rank : (e + 1) * rank], gr[e])
            up = ups + dot32(thin_rows[:, span + e * rank : span + (e + 1) * rank], ur[e])
            hidden = gate / (1.0 + jnp.exp(-gate)) * up * scale
            acc = hidden if acc is None else acc + hidden
            bpart[b, :, e * rank : (e + 1) * rank] = dot32t(hidden.astype(bf16), dl[e])
        hacc[b] = acc
        hsend[b] = acc.astype(bf16)

        @pl.when(jnp.logical_not(root))
        def _():
            h_copy(w, b, d, n).start()

    def b_copy(k):
        return copy(bsend.at[k], brecv.at[k], b_s.at[k], b_r.at[k], "narrow", (pair, across)[k])

    bsend[0] = bpart[...].astype(bf16)
    b_copy(0).start()
    b_copy(0).wait_recv()
    bpart[...] = bpart[...] + brecv[0].astype(f32)
    bsend[1] = bpart[...].astype(bf16)
    b_copy(1).start()
    b_copy(1).wait_recv()
    bfin[...] = (bpart[...] + brecv[1].astype(f32)).astype(bf16)

    def hpair(d):
        b = up_of(count - d)
        return copy(hpl.at[b], hpl.at[b], hb_s.at[0, d], hb_r.at[d], "narrow", pair)

    def hacross(d):
        b = up_of(count - d)
        return copy(hpl.at[b], hpl.at[b], hb_s.at[1, d], hb_r.at[d], "narrow", across)

    for load in loads[4:]:
        load.wait()

    for d in (2, 1, 3, 0):
        b = up_of(count - d)

        @pl.when(root)
        def _():
            whole = hacc[b]
            for k in range(1, count):
                src = up_of(k)
                h_copy(src, b, d, src).wait_recv()
                whole = whole + hrecv[src, b].astype(f32)
            hpl[b] = whole.astype(bf16)
            hacross(d).start()
            hpair(d).start()

        @pl.when(jnp.logical_not(root))
        def _():
            hpair(d).wait_recv()

        @pl.when(relay)
        def _():
            hpair(d).start()

        part = dot32(hpl[b], bd[...]) + dot32(bfin[b], dr[...])
        if d == 0:
            oown[...] = part
        else:
            osend[b] = part.astype(bf16)
            copy(osend.at[b], orecv.at[w], o_s.at[d], o_r.at[d], "wide", b).start()
    total = oown[...]
    for d in (1, 3, 2):
        s = up_of(d)
        copy(osend.at[s], orecv.at[s], o_s.at[d], o_r.at[d], "wide", s).wait_recv()
        total = total + orecv[s].astype(f32)
    out[...] = total.astype(bf16)

    for d in range(1, count):
        b = up_of(count - d)
        tok_copy(d).wait_send()
        wt_copy(d).wait_send()
        ga_copy(d).wait_send()
        copy(gsend.at[b], grecv.at[w], g_s.at[d], g_r.at[d], "wide", b).wait_send()
        copy(osend.at[b], orecv.at[w], o_s.at[d], o_r.at[d], "wide", b).wait_send()
    for k in range(2):
        a_copy(k).wait_send()
        b_copy(k).wait_send()

    @pl.when(root)
    def _():
        for d in range(count):
            src = tok if d == 0 else xcol.at[up_of(count - d)]
            across_copy(d, src).wait_send()
            pair_copy(d, src).wait_send()
            hacross(d).wait_send()
            hpair(d).wait_send()

    @pl.when(relay)
    def _():
        for d in range(count):
            pair_copy(d, xw.at[up_of(count - d)]).wait_send()
            hpair(d).wait_send()

    @pl.when(jnp.logical_not(root))
    def _():
        for d in range(count):
            h_copy(w, up_of(count - d), d, n).wait_send()


def fused(tokens, routes, shares, delta, bg, bu, bd, gl, gr, ul, ur, dl, dr):
    bf16, f32 = jnp.bfloat16, jnp.float32
    count = PLANE
    rows, feats = tokens.shape
    depth, cols = bg.shape
    exp_here, rank, _ = gr.shape
    span = exp_here * rank
    lanes = -(-delta.shape[0] // 128) * 128
    sem = pltpu.SemaphoreType.DMA
    vm = pltpu.VMEM
    out_feats = bd.shape[1]
    vmem, hbm = pl.BlockSpec(memory_space=pltpu.VMEM), pl.BlockSpec(memory_space=pl.ANY)
    return pl.pallas_call(
        kernel,
        out_shape=jax.ShapeDtypeStruct((rows, out_feats), bf16),
        in_specs=[
            vmem, vmem, vmem, pl.BlockSpec(memory_space=pltpu.SMEM),
            hbm, hbm, hbm, hbm, vmem, hbm, vmem, vmem, hbm,
        ],
        out_specs=pl.BlockSpec(memory_space=pltpu.VMEM),
        scratch_shapes=[
            vm((rows, lanes), f32),
            vm((depth, 2 * cols), bf16),
            vm((2 * span, feats), bf16),
            vm(bd.shape, bf16),
            vm((span, out_feats), bf16),
            vm((count, rows, feats), bf16),
            vm((count, rows, feats), bf16),
            vm((count, rows, lanes), f32),
            vm((count, rows, 2 * cols), bf16),
            vm((count, rows, 2 * cols), bf16),
            vm((rows, 2 * cols), f32),
            vm((rows, 2 * cols), bf16),
            vm((count, rows, 2 * cols), bf16),
            vm((count, rows, 2 * span), f32),
            vm((2, count, rows, 2 * span), bf16),
            vm((2, count, rows, 2 * span), bf16),
            vm((count, rows, 2 * span), bf16),
            vm((count, rows, cols), f32),
            vm((count, rows, cols), bf16),
            vm((count, count, rows, cols), bf16),
            vm((count, rows, cols), bf16),
            vm((count, rows, span), f32),
            vm((2, count, rows, span), bf16),
            vm((2, count, rows, span), bf16),
            vm((count, rows, span), bf16),
            vm((count, rows, out_feats), bf16),
            vm((count, rows, out_feats), bf16),
            vm((rows, out_feats), f32),
            sem((count,)), sem((count,)), sem((count,)), sem((count,)),
            sem((count, 2)), sem((count,)),
            sem((count,)), sem((count,)), sem((count,)), sem((count,)),
            sem((2,)), sem((2,)),
            sem((count,)), sem((count, count)), sem((2, count)), sem((count,)),
            sem((2,)), sem((2,)), sem((count,)), sem((count,)), sem((6,)),
        ],
        compiler_params=pltpu.CompilerParams(collective_id=0, has_side_effects=True, vmem_limit_bytes=60 * 1024 * 1024),
    )(
        tokens, routes, shares, delta, bg, bu, bd,
        jnp.swapaxes(gl, 1, 2).reshape(span, feats), gr,
        jnp.swapaxes(ul, 1, 2).reshape(span, feats), ur,
        jnp.swapaxes(dl, 1, 2), dr.reshape(span, out_feats),
    )


def shards(
    tokens,
    routes,
    gate_weights,
    delta_of,
    base_gate,
    base_up,
    base_down,
    gate_left,
    gate_right,
    up_left,
    up_right,
    down_left,
    down_right,
):
    if lax.axis_size("narrow") == PLANE and lax.axis_size("wide") == PLANE:
        return fused(
            tokens, routes, gate_weights, delta_of, base_gate, base_up, base_down,
            gate_left, gate_right, up_left, up_right, down_left, down_right,
        )
    exp_here, _, rank = gate_left.shape
    experts = delta_of.shape[0]
    mine = lax.axis_index("wide")
    bf16 = jnp.bfloat16

    expert_ids = lax.broadcasted_iota(jnp.int32, (1, 1, experts), 2)
    named = routes[:, :, None] == expert_ids
    delta_ids = jnp.sum(jnp.where(named, delta_of[None, None, :], 0), axis=2)
    weight_of = jnp.sum(
        jnp.where(delta_ids[:, :, None] == expert_ids, gate_weights[:, :, None], 0.0), axis=1
    )
    weights = lax.all_gather(weight_of, "wide", axis=0, tiled=True)
    weights = lax.dynamic_slice_in_dim(weights, mine * exp_here, exp_here, axis=1)

    rows = lax.all_gather(tokens, "wide", axis=0, tiled=True)
    full = lax.all_gather(rows, "narrow", axis=1, tiled=True)
    depth = base_gate.shape[0]
    part = lax.dynamic_slice_in_dim(full, mine * depth, depth, axis=1)

    base_both = jnp.concatenate([base_gate, base_up], axis=1)
    both = lax.psum(dot32(part, base_both), "wide")
    columns = base_gate.shape[1]

    lefts = jnp.concatenate([gate_left, up_left], axis=0)
    low = lax.psum(jnp.einsum("td,edr->ter", rows, lefts, preferred_element_type=jnp.float32), "narrow")
    low = low.astype(bf16)

    mixed = 0.0
    thin = []
    for e in range(exp_here):
        gate = both[:, :columns] + dot32(low[:, e], gate_right[e])
        up = both[:, columns:] + dot32(low[:, exp_here + e], up_right[e])
        hidden = jax.nn.silu(gate) * up * weights[:, e : e + 1]
        mixed = mixed + hidden
        thin.append(dot32(hidden.astype(bf16), down_left[e]))
    mixed = lax.psum(mixed, "wide").astype(bf16)
    mixed_full = lax.all_gather(mixed, "narrow", axis=1, tiled=True)
    depth = base_down.shape[0]
    mixed_part = lax.dynamic_slice_in_dim(mixed_full, mine * depth, depth, axis=1)
    thin = lax.psum(jnp.concatenate(thin, axis=1), "narrow").astype(bf16)
    out = dot32(mixed_part, base_down) + dot32(thin, down_right.reshape(exp_here * rank, -1))
    out = lax.psum_scatter(out, "wide", scatter_dimension=0, tiled=True)
    return out.astype(bf16)


def solution(mesh):
    return jax.shard_map(
        shards,
        mesh=mesh,
        in_specs=(
            P(("groups", "wide"), "narrow"),
            P(("groups", "wide"), None),
            P(("groups", "wide"), None),
            P(),
            P("wide", "narrow"),
            P("wide", "narrow"),
            P("wide", "narrow"),
            P("wide", "narrow", None),
            P("wide", None, "narrow"),
            P("wide", "narrow", None),
            P("wide", None, "narrow"),
            P("wide", "narrow", None),
            P("wide", None, "narrow"),
        ),
        out_specs=P(("groups", "wide"), "narrow"),
        check_vma=False,
    )
```

```python
import jax
import jax.numpy as jnp
from jax import lax
from jax.experimental import pallas as pl
from jax.experimental.pallas import tpu as pltpu
from jax.sharding import PartitionSpec as P


def dot32(a, b):
    return jnp.dot(a, b, preferred_element_type=jnp.float32)


def dot32t(a, b):
    return lax.dot_general(a, b, (((1,), (1,)), ((), ())), preferred_element_type=jnp.float32)


PLANE = 4

LANES = 128


def kernel(
    tok, routes, shares, delta, bg_hbm, bu_hbm, bd_hbm, gl_hbm, gr, ul_hbm, ur, dl, dr_hbm, out,
    wt, bgu, lefts, bd, dr,
    xcol, xw, wts, gsend, grecv, gown, gred, gall, apart, asend, arecv, afin,
    hacc, hsend, hrecv, hpl, bpart, bsend, brecv, bfin, osend, orecv, oown,
    tok_s, tok_r, wt_s, wt_r, bs_s, bs_r, g_s, g_r, ga_s, ga_r, a_s, a_r,
    h_s, h_r, hb_s, hb_r, b_s, b_r, o_s, o_r, in_s,
):
    bf16, f32 = jnp.bfloat16, jnp.float32
    count = PLANE
    w, n = lax.axis_index("wide"), lax.axis_index("narrow")
    exp_here, rank, cols = gr.shape
    span = exp_here * rank
    loads = [
        pltpu.make_async_copy(gl_hbm, lefts.at[pl.ds(0, span)], in_s.at[0]),
        pltpu.make_async_copy(ul_hbm, lefts.at[pl.ds(span, span)], in_s.at[1]),
    ]
    chunk = LANES if cols % LANES == 0 else cols
    chunks = cols // chunk
    for c in range(chunks):
        for k, base in enumerate((bg_hbm, bu_hbm)):
            place = bgu.at[:, pl.ds((2 * c + k) * chunk, chunk)]
            loads.append(pltpu.make_async_copy(base.at[:, pl.ds(c * chunk, chunk)], place, in_s.at[2 + 2 * c + k]))
    loads.append(pltpu.make_async_copy(bd_hbm, bd, in_s.at[2 + 2 * chunks]))
    loads.append(pltpu.make_async_copy(dr_hbm, dr, in_s.at[3 + 2 * chunks]))
    for load in loads:
        load.start()
    pair = n + 1 - 2 * lax.rem(n, 2)
    across = lax.rem(n + 2, count)
    root = n == w
    relay = n == lax.rem(w + 2, count)

    def up_of(d):
        return lax.rem(w + d, count)

    def copy(src, dst, ss, rs, axis, peer):
        return pltpu.make_async_remote_copy(
            src_ref=src, dst_ref=dst, send_sem=ss, recv_sem=rs,
            device_id={axis: peer}, device_id_type=pl.DeviceIdType.MESH,
        )

    barrier = pltpu.get_barrier_semaphore()
    for d in range(1, count):
        pl.semaphore_signal(barrier, inc=1, device_id={"wide": up_of(d)}, device_id_type=pl.DeviceIdType.MESH)
    for peer in (pair, across):
        pl.semaphore_signal(barrier, inc=1, device_id={"narrow": peer}, device_id_type=pl.DeviceIdType.MESH)
    pl.semaphore_wait(barrier, count + 1)

    def tok_copy(d):
        return copy(tok, xcol.at[w], tok_s.at[d], tok_r.at[d], "wide", up_of(d))

    def wt_copy(d):
        return copy(wt, wts.at[w], wt_s.at[d], wt_r.at[d], "wide", up_of(d))

    def pair_copy(d, src):
        return copy(src, xw.at[up_of(count - d)], bs_s.at[d, 0], bs_r.at[d], "narrow", pair)

    def across_copy(d, src):
        return copy(src, xw.at[up_of(count - d)], bs_s.at[d, 1], bs_r.at[d], "narrow", across)

    for d in range(1, count):
        tok_copy(d).start()

    def g_copy(d, c, peer, slot):
        part = pl.ds(2 * c * chunk, 2 * chunk)
        return copy(gsend.at[peer, :, part], grecv.at[slot, :, part], g_s.at[d, c], g_r.at[d, c], "wide", peer)

    named, ids = routes[...], jnp.zeros(routes.shape, jnp.int32)
    for e in range(delta.shape[0]):
        ids = jnp.where(named == e, delta[e], ids)
    sets = lax.broadcasted_iota(jnp.int32, (wt.shape[1], wt.shape[0]), 0)
    table = jnp.zeros(sets.shape, f32)
    for k in range(routes.shape[0]):
        table = table + jnp.where(sets == ids[k : k + 1], shares[k : k + 1, :], 0.0)
    wt[...] = table.T
    for load in loads[:-2]:
        load.wait()

    def low(rows, b):
        apart[b] = dot32t(rows, lefts[...])

    for d in range(count):
        b = up_of(count - d)
        if d > 0:
            tok_copy(d).wait_recv()
        mine = tok if d == 0 else xcol.at[b]

        @pl.when(root)
        def _():
            across_copy(d, mine).start()
            pair_copy(d, mine).start()
            xw[b] = mine[...]

        low(mine[...], b)

        @pl.when(jnp.logical_not(root))
        def _():
            pair_copy(d, xw.at[b]).wait_recv()

        @pl.when(relay)
        def _():
            pair_copy(d, xw.at[b]).start()

        rows = xw[b]
        both = dot32(rows, bgu[...])
        if d == 0:
            gown[...] = both
            for k in range(1, count):
                wt_copy(k).start()
        else:
            gsend[b] = both.astype(bf16)
            for c in range(chunks):
                g_copy(d, c, b, w).start()

    def a_copy(k):
        return copy(asend.at[k], arecv.at[k], a_s.at[k], a_r.at[k], "narrow", (pair, across)[k])

    asend[0] = apart[...].astype(bf16)
    a_copy(0).start()
    a_copy(0).wait_recv()
    apart[...] = apart[...] + arecv[0].astype(f32)
    asend[1] = apart[...].astype(bf16)
    a_copy(1).start()

    def ga_copy(d, c):
        part = pl.ds(2 * c * chunk, 2 * chunk)
        return copy(gred.at[:, part], gall.at[w, :, part], ga_s.at[d, c], ga_r.at[d, c], "wide", up_of(d))

    for c in range(chunks):
        part = slice(2 * c * chunk, 2 * (c + 1) * chunk)
        total = gown[:, part]
        for d in range(1, count):
            g_copy(d, c, up_of(d), up_of(d)).wait_recv()
            total = total + grecv[up_of(d), :, part].astype(f32)
        gown[:, part] = total
        gred[:, part] = total.astype(bf16)
        for d in range(1, count):
            ga_copy(d, c).start()

    a_copy(1).wait_recv()
    afin[...] = (apart[...] + arecv[1].astype(f32)).astype(bf16)

    def h_copy(slot, c, target):
        part = pl.ds(c * chunk, chunk)
        return copy(hsend.at[:, :, part], hrecv.at[slot, :, :, part], h_s.at[c], h_r.at[slot, c], "wide", target)

    for c in range(chunks):
        gate_part = slice(2 * c * chunk, (2 * c + 1) * chunk)
        up_part = slice((2 * c + 1) * chunk, 2 * (c + 1) * chunk)
        part = slice(c * chunk, (c + 1) * chunk)
        for d in range(count):
            b = up_of(count - d)
            if d > 0:
                ga_copy(d, c).wait_recv()
                if c == 0:
                    wt_copy(d).wait_recv()
                gates, ups = gall[b, :, gate_part].astype(f32), gall[b, :, up_part].astype(f32)
                scales = wts[b]
            else:
                gates, ups = gown[:, gate_part], gown[:, up_part]
                scales = wt[...]
            ids = lax.broadcasted_iota(jnp.int32, scales.shape, 1)
            thin_rows = afin[b]
            acc = None
            for e in range(exp_here):
                scale = jnp.sum(jnp.where(ids == w * exp_here + e, scales, 0.0), axis=1, keepdims=True)
                own = slice(e * rank, (e + 1) * rank)
                gate = gates + dot32(thin_rows[:, own], gr[e, :, part])
                up = ups + dot32(thin_rows[:, span + e * rank : span + (e + 1) * rank], ur[e, :, part])
                hidden = gate / (1.0 + jnp.exp(-gate)) * up * scale
                acc = hidden if acc is None else acc + hidden
                thin = dot32t(hidden.astype(bf16), dl[e, :, part])
                bpart[b, :, own] = thin if c == 0 else bpart[b, :, own] + thin
            hacc[b, :, part] = acc
            hsend[b, :, part] = acc.astype(bf16)

        @pl.when(jnp.logical_not(root))
        def _():
            h_copy(w, c, n).start()

    def b_copy(k):
        return copy(bsend.at[k], brecv.at[k], b_s.at[k], b_r.at[k], "narrow", (pair, across)[k])

    bsend[0] = bpart[...].astype(bf16)
    b_copy(0).start()
    b_copy(0).wait_recv()
    bpart[...] = bpart[...] + brecv[0].astype(f32)
    bsend[1] = bpart[...].astype(bf16)
    b_copy(1).start()
    b_copy(1).wait_recv()
    bfin[...] = (bpart[...] + brecv[1].astype(f32)).astype(bf16)

    def hpair(d):
        b = up_of(count - d)
        return copy(hpl.at[b], hpl.at[b], hb_s.at[0, d], hb_r.at[d], "narrow", pair)

    def hacross(d):
        b = up_of(count - d)
        return copy(hpl.at[b], hpl.at[b], hb_s.at[1, d], hb_r.at[d], "narrow", across)

    for load in loads[-2:]:
        load.wait()

    for d in (2, 1, 3, 0):
        b = up_of(count - d)

        @pl.when(root)
        def _():
            whole = hacc[b]
            for k in range(1, count):
                src = up_of(k)
                if d == 2:
                    for c in range(chunks):
                        h_copy(src, c, src).wait_recv()
                whole = whole + hrecv[src, b].astype(f32)
            hpl[b] = whole.astype(bf16)
            hacross(d).start()
            hpair(d).start()

        @pl.when(jnp.logical_not(root))
        def _():
            hpair(d).wait_recv()

        @pl.when(relay)
        def _():
            hpair(d).start()

        part = dot32(hpl[b], bd[...]) + dot32(bfin[b], dr[...])
        if d == 0:
            oown[...] = part
        else:
            osend[b] = part.astype(bf16)
            copy(osend.at[b], orecv.at[w], o_s.at[d], o_r.at[d], "wide", b).start()
    total = oown[...]
    for d in (1, 3, 2):
        s = up_of(d)
        copy(osend.at[s], orecv.at[s], o_s.at[d], o_r.at[d], "wide", s).wait_recv()
        total = total + orecv[s].astype(f32)
    out[...] = total.astype(bf16)

    for d in range(1, count):
        b = up_of(count - d)
        tok_copy(d).wait_send()
        wt_copy(d).wait_send()
        for c in range(chunks):
            ga_copy(d, c).wait_send()
            g_copy(d, c, b, w).wait_send()
        copy(osend.at[b], orecv.at[w], o_s.at[d], o_r.at[d], "wide", b).wait_send()
    for k in range(2):
        a_copy(k).wait_send()
        b_copy(k).wait_send()

    @pl.when(root)
    def _():
        for d in range(count):
            src = tok if d == 0 else xcol.at[up_of(count - d)]
            across_copy(d, src).wait_send()
            pair_copy(d, src).wait_send()
            hacross(d).wait_send()
            hpair(d).wait_send()

    @pl.when(relay)
    def _():
        for d in range(count):
            pair_copy(d, xw.at[up_of(count - d)]).wait_send()
            hpair(d).wait_send()

    @pl.when(jnp.logical_not(root))
    def _():
        for c in range(chunks):
            h_copy(w, c, n).wait_send()


def fused(tokens, routes, shares, delta, bg, bu, bd, gl, gr, ul, ur, dl, dr):
    bf16, f32 = jnp.bfloat16, jnp.float32
    count = PLANE
    rows, feats = tokens.shape
    depth, cols = bg.shape
    exp_here, rank, _ = gr.shape
    span = exp_here * rank
    lanes = -(-delta.shape[0] // LANES) * LANES
    chunks = cols // LANES if cols % LANES == 0 else 1
    sem = pltpu.SemaphoreType.DMA
    vm = pltpu.VMEM
    out_feats = bd.shape[1]
    vmem, hbm = pl.BlockSpec(memory_space=pltpu.VMEM), pl.BlockSpec(memory_space=pl.ANY)
    return pl.pallas_call(
        kernel,
        out_shape=jax.ShapeDtypeStruct((rows, out_feats), bf16),
        in_specs=[
            vmem, vmem, vmem, pl.BlockSpec(memory_space=pltpu.SMEM),
            hbm, hbm, hbm, hbm, vmem, hbm, vmem, vmem, hbm,
        ],
        out_specs=pl.BlockSpec(memory_space=pltpu.VMEM),
        scratch_shapes=[
            vm((rows, lanes), f32),
            vm((depth, 2 * cols), bf16),
            vm((2 * span, feats), bf16),
            vm(bd.shape, bf16),
            vm((span, out_feats), bf16),
            vm((count, rows, feats), bf16),
            vm((count, rows, feats), bf16),
            vm((count, rows, lanes), f32),
            vm((count, rows, 2 * cols), bf16),
            vm((count, rows, 2 * cols), bf16),
            vm((rows, 2 * cols), f32),
            vm((rows, 2 * cols), bf16),
            vm((count, rows, 2 * cols), bf16),
            vm((count, rows, 2 * span), f32),
            vm((2, count, rows, 2 * span), bf16),
            vm((2, count, rows, 2 * span), bf16),
            vm((count, rows, 2 * span), bf16),
            vm((count, rows, cols), f32),
            vm((count, rows, cols), bf16),
            vm((count, count, rows, cols), bf16),
            vm((count, rows, cols), bf16),
            vm((count, rows, span), f32),
            vm((2, count, rows, span), bf16),
            vm((2, count, rows, span), bf16),
            vm((count, rows, span), bf16),
            vm((count, rows, out_feats), bf16),
            vm((count, rows, out_feats), bf16),
            vm((rows, out_feats), f32),
            sem((count,)), sem((count,)), sem((count,)), sem((count,)),
            sem((count, 2)), sem((count,)),
            sem((count, chunks)), sem((count, chunks)), sem((count, chunks)), sem((count, chunks)),
            sem((2,)), sem((2,)),
            sem((chunks,)), sem((count, chunks)), sem((2, count)), sem((count,)),
            sem((2,)), sem((2,)), sem((count,)), sem((count,)), sem((4 + 2 * chunks,)),
        ],
        compiler_params=pltpu.CompilerParams(collective_id=0, has_side_effects=True, vmem_limit_bytes=60 * 1024 * 1024),
    )(
        tokens, routes.T, shares.T, delta, bg, bu, bd,
        jnp.swapaxes(gl, 1, 2).reshape(span, feats), gr,
        jnp.swapaxes(ul, 1, 2).reshape(span, feats), ur,
        jnp.swapaxes(dl, 1, 2), dr.reshape(span, out_feats),
    )


def shards(
    tokens,
    routes,
    gate_weights,
    delta_of,
    base_gate,
    base_up,
    base_down,
    gate_left,
    gate_right,
    up_left,
    up_right,
    down_left,
    down_right,
):
    if lax.axis_size("narrow") == PLANE and lax.axis_size("wide") == PLANE:
        return fused(
            tokens, routes, gate_weights, delta_of, base_gate, base_up, base_down,
            gate_left, gate_right, up_left, up_right, down_left, down_right,
        )
    exp_here, _, rank = gate_left.shape
    experts = delta_of.shape[0]
    mine = lax.axis_index("wide")
    bf16 = jnp.bfloat16

    expert_ids = lax.broadcasted_iota(jnp.int32, (1, 1, experts), 2)
    named = routes[:, :, None] == expert_ids
    delta_ids = jnp.sum(jnp.where(named, delta_of[None, None, :], 0), axis=2)
    weight_of = jnp.sum(
        jnp.where(delta_ids[:, :, None] == expert_ids, gate_weights[:, :, None], 0.0), axis=1
    )
    weights = lax.all_gather(weight_of, "wide", axis=0, tiled=True)
    weights = lax.dynamic_slice_in_dim(weights, mine * exp_here, exp_here, axis=1)

    rows = lax.all_gather(tokens, "wide", axis=0, tiled=True)
    full = lax.all_gather(rows, "narrow", axis=1, tiled=True)
    depth = base_gate.shape[0]
    part = lax.dynamic_slice_in_dim(full, mine * depth, depth, axis=1)

    base_both = jnp.concatenate([base_gate, base_up], axis=1)
    both = lax.psum(dot32(part, base_both), "wide")
    columns = base_gate.shape[1]

    lefts = jnp.concatenate([gate_left, up_left], axis=0)
    low = lax.psum(jnp.einsum("td,edr->ter", rows, lefts, preferred_element_type=jnp.float32), "narrow")
    low = low.astype(bf16)

    mixed = 0.0
    thin = []
    for e in range(exp_here):
        gate = both[:, :columns] + dot32(low[:, e], gate_right[e])
        up = both[:, columns:] + dot32(low[:, exp_here + e], up_right[e])
        hidden = jax.nn.silu(gate) * up * weights[:, e : e + 1]
        mixed = mixed + hidden
        thin.append(dot32(hidden.astype(bf16), down_left[e]))
    mixed = lax.psum(mixed, "wide").astype(bf16)
    mixed_full = lax.all_gather(mixed, "narrow", axis=1, tiled=True)
    depth = base_down.shape[0]
    mixed_part = lax.dynamic_slice_in_dim(mixed_full, mine * depth, depth, axis=1)
    thin = lax.psum(jnp.concatenate(thin, axis=1), "narrow").astype(bf16)
    out = dot32(mixed_part, base_down) + dot32(thin, down_right.reshape(exp_here * rank, -1))
    out = lax.psum_scatter(out, "wide", scatter_dimension=0, tiled=True)
    return out.astype(bf16)


def solution(mesh):
    return jax.shard_map(
        shards,
        mesh=mesh,
        in_specs=(
            P(("groups", "wide"), "narrow"),
            P(("groups", "wide"), None),
            P(("groups", "wide"), None),
            P(),
            P("wide", "narrow"),
            P("wide", "narrow"),
            P("wide", "narrow"),
            P("wide", "narrow", None),
            P("wide", None, "narrow"),
            P("wide", "narrow", None),
            P("wide", None, "narrow"),
            P("wide", "narrow", None),
            P("wide", None, "narrow"),
        ),
        out_specs=P(("groups", "wide"), "narrow"),
        check_vma=False,
    )
```

```python
import functools

import jax
import jax.numpy as jnp
from jax import lax
from jax.experimental import pallas as pl
from jax.experimental.pallas import tpu as pltpu
from jax.sharding import PartitionSpec as P


def dot32(a, b):
    return jnp.dot(a, b, preferred_element_type=jnp.float32)


def dot32t(a, b):
    return lax.dot_general(a, b, (((1,), (1,)), ((), ())), preferred_element_type=jnp.float32)


PLANE = 4

LANES = 128


def kernel(
    tok, routes, shares, delta, bg_hbm, bu_hbm, bd_hbm, gl_hbm, gr, ul_hbm, ur, dl, dr_hbm, out,
    wt, bgu, lefts, bd, dr,
    xcol, xw, wts, gsend, grecv, gown, gred, gall, apart, asend, arecv, afin,
    hacc, hsend, hrecv, hpl, bpart, bsend, brecv, bfin, osend, orecv, oown,
    tok_s, tok_r, wt_s, wt_r, bs_s, bs_r, g_s, g_r, ga_s, ga_r, a_s, a_r,
    h_s, h_r, hb_s, hb_r, b_s, b_r, o_s, o_r, in_s,
):
    bf16, f32 = jnp.bfloat16, jnp.float32
    count = PLANE
    w, n = lax.axis_index("wide"), lax.axis_index("narrow")
    exp_here, rank, cols = gr.shape
    span = exp_here * rank
    loads = [
        pltpu.make_async_copy(gl_hbm, lefts.at[pl.ds(0, span)], in_s.at[0]),
        pltpu.make_async_copy(ul_hbm, lefts.at[pl.ds(span, span)], in_s.at[1]),
    ]
    chunk = LANES if cols % LANES == 0 else cols
    chunks = cols // chunk
    for c in range(chunks):
        for k, base in enumerate((bg_hbm, bu_hbm)):
            place = bgu.at[:, pl.ds((2 * c + k) * chunk, chunk)]
            loads.append(pltpu.make_async_copy(base.at[:, pl.ds(c * chunk, chunk)], place, in_s.at[2 + 2 * c + k]))
    loads.append(pltpu.make_async_copy(bd_hbm, bd, in_s.at[2 + 2 * chunks]))
    loads.append(pltpu.make_async_copy(dr_hbm, dr, in_s.at[3 + 2 * chunks]))
    for load in loads:
        load.start()
    pair = n + 1 - 2 * lax.rem(n, 2)
    across = lax.rem(n + 2, count)
    root = n == w
    relay = n == lax.rem(w + 2, count)

    def up_of(d):
        return lax.rem(w + d, count)

    def copy(src, dst, ss, rs, axis, peer):
        return pltpu.make_async_remote_copy(
            src_ref=src, dst_ref=dst, send_sem=ss, recv_sem=rs,
            device_id={axis: peer}, device_id_type=pl.DeviceIdType.MESH,
        )

    barrier = pltpu.get_barrier_semaphore()
    for d in range(1, count):
        pl.semaphore_signal(barrier, inc=1, device_id={"wide": up_of(d)}, device_id_type=pl.DeviceIdType.MESH)
    for peer in (pair, across):
        pl.semaphore_signal(barrier, inc=1, device_id={"narrow": peer}, device_id_type=pl.DeviceIdType.MESH)
    pl.semaphore_wait(barrier, count + 1)

    def tok_copy(way, hop):
        peer = up_of((1, count - 1)[way])
        block = up_of((count - hop + 1, hop - 1)[way])
        src = tok if hop == 1 else xcol.at[block]
        return copy(src, xcol.at[block], tok_s.at[way, hop], tok_r.at[way, hop], "wide", peer)

    def open_way(way):
        return (w < count - 1, w > 0)[way]

    def reaches(way, hop):
        return (w >= hop, w + hop < count)[way]

    visits = [(0, 0, None)] + [(hop, way, reaches(way, hop)) for hop in range(1, count) for way in range(2)]

    def block_of(hop, way):
        return up_of(((count - hop) % count, hop)[way])

    def wt_copy(d):
        return copy(wt, wts.at[w], wt_s.at[d], wt_r.at[d], "wide", up_of(d))

    def pair_copy(b, src):
        return copy(src, xw.at[b], bs_s.at[b, 0], bs_r.at[b], "narrow", pair)

    def across_copy(b, src):
        return copy(src, xw.at[b], bs_s.at[b, 1], bs_r.at[b], "narrow", across)

    for way in range(2):

        @pl.when(open_way(way))
        def _():
            tok_copy(way, 1).start()

    def g_copy(d, c, peer, slot):
        part = pl.ds(2 * c * chunk, 2 * chunk)
        return copy(gsend.at[peer, :, part], grecv.at[slot, :, part], g_s.at[d, c], g_r.at[d, c], "wide", peer)

    named, ids = routes[...], jnp.zeros(routes.shape, jnp.int32)
    for e in range(delta.shape[0]):
        ids = jnp.where(named == e, delta[e], ids)
    sets = lax.broadcasted_iota(jnp.int32, (wt.shape[1], wt.shape[0]), 0)
    table = jnp.zeros(sets.shape, f32)
    for k in range(routes.shape[0]):
        table = table + jnp.where(sets == ids[k : k + 1], shares[k : k + 1, :], 0.0)
    wt[...] = table.T
    for load in loads[:-2]:
        load.wait()

    def low(rows, b):
        apart[b] = dot32t(rows, lefts[...])

    def visit(hop, way):
        b = block_of(hop, way)
        mine = tok if hop == 0 else xcol.at[b]
        if hop > 0:
            tok_copy(way, hop).wait_recv()
        if 0 < hop < count - 1:

            @pl.when(open_way(way))
            def _():
                tok_copy(way, hop + 1).start()

        @pl.when(root)
        def _():
            across_copy(b, mine).start()
            pair_copy(b, mine).start()
            xw[b] = mine[...]

        low(mine[...], b)

        @pl.when(jnp.logical_not(root))
        def _():
            pair_copy(b, xw.at[b]).wait_recv()

        @pl.when(relay)
        def _():
            pair_copy(b, xw.at[b]).start()

        both = dot32(xw[b], bgu[...])
        if hop == 0:
            gown[...] = both
            for k in range(1, count):
                wt_copy(k).start()
        else:
            gsend[b] = both.astype(bf16)
            for c in range(chunks):
                g_copy((hop, count - hop)[way], c, b, w).start()

    for hop, way, there in visits:
        if there is None:
            visit(hop, way)
        else:
            pl.when(there)(functools.partial(visit, hop, way))

    def a_copy(k):
        return copy(asend.at[k], arecv.at[k], a_s.at[k], a_r.at[k], "narrow", (pair, across)[k])

    asend[0] = apart[...].astype(bf16)
    a_copy(0).start()
    a_copy(0).wait_recv()
    apart[...] = apart[...] + arecv[0].astype(f32)
    asend[1] = apart[...].astype(bf16)
    a_copy(1).start()

    def ga_copy(d, c):
        part = pl.ds(2 * c * chunk, 2 * chunk)
        return copy(gred.at[:, part], gall.at[w, :, part], ga_s.at[d, c], ga_r.at[d, c], "wide", up_of(d))

    for c in range(chunks):
        part = slice(2 * c * chunk, 2 * (c + 1) * chunk)
        total = gown[:, part]
        for d in range(1, count):
            g_copy(d, c, up_of(d), up_of(d)).wait_recv()
            total = total + grecv[up_of(d), :, part].astype(f32)
        gown[:, part] = total
        gred[:, part] = total.astype(bf16)
        for d in range(1, count):
            ga_copy(d, c).start()

    a_copy(1).wait_recv()
    afin[...] = (apart[...] + arecv[1].astype(f32)).astype(bf16)

    def h_copy(slot, c, target):
        part = pl.ds(c * chunk, chunk)
        return copy(hsend.at[:, :, part], hrecv.at[slot, :, :, part], h_s.at[c], h_r.at[slot, c], "wide", target)

    for c in range(chunks):
        gate_part = slice(2 * c * chunk, (2 * c + 1) * chunk)
        up_part = slice((2 * c + 1) * chunk, 2 * (c + 1) * chunk)
        part = slice(c * chunk, (c + 1) * chunk)
        for d in range(count):
            b = up_of(count - d)
            if d > 0:
                ga_copy(d, c).wait_recv()
                if c == 0:
                    wt_copy(d).wait_recv()
                gates, ups = gall[b, :, gate_part].astype(f32), gall[b, :, up_part].astype(f32)
                scales = wts[b]
            else:
                gates, ups = gown[:, gate_part], gown[:, up_part]
                scales = wt[...]
            ids = lax.broadcasted_iota(jnp.int32, scales.shape, 1)
            thin_rows = afin[b]
            acc = None
            for e in range(exp_here):
                scale = jnp.sum(jnp.where(ids == w * exp_here + e, scales, 0.0), axis=1, keepdims=True)
                own = slice(e * rank, (e + 1) * rank)
                gate = gates + dot32(thin_rows[:, own], gr[e, :, part])
                up = ups + dot32(thin_rows[:, span + e * rank : span + (e + 1) * rank], ur[e, :, part])
                hidden = gate / (1.0 + jnp.exp(-gate)) * up * scale
                acc = hidden if acc is None else acc + hidden
                thin = dot32t(hidden.astype(bf16), dl[e, :, part])
                bpart[b, :, own] = thin if c == 0 else bpart[b, :, own] + thin
            hacc[b, :, part] = acc
            hsend[b, :, part] = acc.astype(bf16)

        @pl.when(jnp.logical_not(root))
        def _():
            h_copy(w, c, n).start()

    def b_copy(k):
        return copy(bsend.at[k], brecv.at[k], b_s.at[k], b_r.at[k], "narrow", (pair, across)[k])

    bsend[0] = bpart[...].astype(bf16)
    b_copy(0).start()
    b_copy(0).wait_recv()
    bpart[...] = bpart[...] + brecv[0].astype(f32)
    bsend[1] = bpart[...].astype(bf16)
    b_copy(1).start()
    b_copy(1).wait_recv()
    bfin[...] = (bpart[...] + brecv[1].astype(f32)).astype(bf16)

    def hpair(d):
        b = up_of(count - d)
        return copy(hpl.at[b], hpl.at[b], hb_s.at[0, d], hb_r.at[d], "narrow", pair)

    def hacross(d):
        b = up_of(count - d)
        return copy(hpl.at[b], hpl.at[b], hb_s.at[1, d], hb_r.at[d], "narrow", across)

    for load in loads[-2:]:
        load.wait()

    for d in (2, 1, 3, 0):
        b = up_of(count - d)

        @pl.when(root)
        def _():
            whole = hacc[b]
            for k in range(1, count):
                src = up_of(k)
                if d == 2:
                    for c in range(chunks):
                        h_copy(src, c, src).wait_recv()
                whole = whole + hrecv[src, b].astype(f32)
            hpl[b] = whole.astype(bf16)
            hacross(d).start()
            hpair(d).start()

        @pl.when(jnp.logical_not(root))
        def _():
            hpair(d).wait_recv()

        @pl.when(relay)
        def _():
            hpair(d).start()

        part = dot32(hpl[b], bd[...]) + dot32(bfin[b], dr[...])
        if d == 0:
            oown[...] = part
        else:
            osend[b] = part.astype(bf16)
            copy(osend.at[b], orecv.at[w], o_s.at[d], o_r.at[d], "wide", b).start()
    total = oown[...]
    for d in (1, 3, 2):
        s = up_of(d)
        copy(osend.at[s], orecv.at[s], o_s.at[d], o_r.at[d], "wide", s).wait_recv()
        total = total + orecv[s].astype(f32)
    out[...] = total.astype(bf16)

    for d in range(1, count):
        b = up_of(count - d)
        wt_copy(d).wait_send()
        for c in range(chunks):
            ga_copy(d, c).wait_send()
            g_copy(d, c, b, w).wait_send()
        copy(osend.at[b], orecv.at[w], o_s.at[d], o_r.at[d], "wide", b).wait_send()
    for way in range(2):

        @pl.when(open_way(way))
        def _():
            tok_copy(way, 1).wait_send()

        for hop in range(1, count - 1):

            @pl.when(jnp.logical_and(open_way(way), reaches(way, hop)))
            def _():
                tok_copy(way, hop + 1).wait_send()

    for k in range(2):
        a_copy(k).wait_send()
        b_copy(k).wait_send()

    @pl.when(root)
    def _():
        for d in range(count):
            b = up_of(count - d)
            src = tok if d == 0 else xcol.at[b]
            across_copy(b, src).wait_send()
            pair_copy(b, src).wait_send()
            hacross(d).wait_send()
            hpair(d).wait_send()

    @pl.when(relay)
    def _():
        for d in range(count):
            b = up_of(count - d)
            pair_copy(b, xw.at[b]).wait_send()
            hpair(d).wait_send()

    @pl.when(jnp.logical_not(root))
    def _():
        for c in range(chunks):
            h_copy(w, c, n).wait_send()


def fused(tokens, routes, shares, delta, bg, bu, bd, gl, gr, ul, ur, dl, dr):
    bf16, f32 = jnp.bfloat16, jnp.float32
    count = PLANE
    rows, feats = tokens.shape
    depth, cols = bg.shape
    exp_here, rank, _ = gr.shape
    span = exp_here * rank
    lanes = -(-delta.shape[0] // LANES) * LANES
    chunks = cols // LANES if cols % LANES == 0 else 1
    sem = pltpu.SemaphoreType.DMA
    vm = pltpu.VMEM
    out_feats = bd.shape[1]
    vmem, hbm = pl.BlockSpec(memory_space=pltpu.VMEM), pl.BlockSpec(memory_space=pl.ANY)
    return pl.pallas_call(
        kernel,
        out_shape=jax.ShapeDtypeStruct((rows, out_feats), bf16),
        in_specs=[
            vmem, vmem, vmem, pl.BlockSpec(memory_space=pltpu.SMEM),
            hbm, hbm, hbm, hbm, vmem, hbm, vmem, vmem, hbm,
        ],
        out_specs=pl.BlockSpec(memory_space=pltpu.VMEM),
        scratch_shapes=[
            vm((rows, lanes), f32),
            vm((depth, 2 * cols), bf16),
            vm((2 * span, feats), bf16),
            vm(bd.shape, bf16),
            vm((span, out_feats), bf16),
            vm((count, rows, feats), bf16),
            vm((count, rows, feats), bf16),
            vm((count, rows, lanes), f32),
            vm((count, rows, 2 * cols), bf16),
            vm((count, rows, 2 * cols), bf16),
            vm((rows, 2 * cols), f32),
            vm((rows, 2 * cols), bf16),
            vm((count, rows, 2 * cols), bf16),
            vm((count, rows, 2 * span), f32),
            vm((2, count, rows, 2 * span), bf16),
            vm((2, count, rows, 2 * span), bf16),
            vm((count, rows, 2 * span), bf16),
            vm((count, rows, cols), f32),
            vm((count, rows, cols), bf16),
            vm((count, count, rows, cols), bf16),
            vm((count, rows, cols), bf16),
            vm((count, rows, span), f32),
            vm((2, count, rows, span), bf16),
            vm((2, count, rows, span), bf16),
            vm((count, rows, span), bf16),
            vm((count, rows, out_feats), bf16),
            vm((count, rows, out_feats), bf16),
            vm((rows, out_feats), f32),
            sem((2, count)), sem((2, count)), sem((count,)), sem((count,)),
            sem((count, 2)), sem((count,)),
            sem((count, chunks)), sem((count, chunks)), sem((count, chunks)), sem((count, chunks)),
            sem((2,)), sem((2,)),
            sem((chunks,)), sem((count, chunks)), sem((2, count)), sem((count,)),
            sem((2,)), sem((2,)), sem((count,)), sem((count,)), sem((4 + 2 * chunks,)),
        ],
        compiler_params=pltpu.CompilerParams(collective_id=0, has_side_effects=True, vmem_limit_bytes=60 * 1024 * 1024),
    )(
        tokens, routes.T, shares.T, delta, bg, bu, bd,
        jnp.swapaxes(gl, 1, 2).reshape(span, feats), gr,
        jnp.swapaxes(ul, 1, 2).reshape(span, feats), ur,
        jnp.swapaxes(dl, 1, 2), dr.reshape(span, out_feats),
    )


def shards(
    tokens,
    routes,
    gate_weights,
    delta_of,
    base_gate,
    base_up,
    base_down,
    gate_left,
    gate_right,
    up_left,
    up_right,
    down_left,
    down_right,
):
    if lax.axis_size("narrow") == PLANE and lax.axis_size("wide") == PLANE:
        return fused(
            tokens, routes, gate_weights, delta_of, base_gate, base_up, base_down,
            gate_left, gate_right, up_left, up_right, down_left, down_right,
        )
    exp_here, _, rank = gate_left.shape
    experts = delta_of.shape[0]
    mine = lax.axis_index("wide")
    bf16 = jnp.bfloat16

    expert_ids = lax.broadcasted_iota(jnp.int32, (1, 1, experts), 2)
    named = routes[:, :, None] == expert_ids
    delta_ids = jnp.sum(jnp.where(named, delta_of[None, None, :], 0), axis=2)
    weight_of = jnp.sum(
        jnp.where(delta_ids[:, :, None] == expert_ids, gate_weights[:, :, None], 0.0), axis=1
    )
    weights = lax.all_gather(weight_of, "wide", axis=0, tiled=True)
    weights = lax.dynamic_slice_in_dim(weights, mine * exp_here, exp_here, axis=1)

    rows = lax.all_gather(tokens, "wide", axis=0, tiled=True)
    full = lax.all_gather(rows, "narrow", axis=1, tiled=True)
    depth = base_gate.shape[0]
    part = lax.dynamic_slice_in_dim(full, mine * depth, depth, axis=1)

    base_both = jnp.concatenate([base_gate, base_up], axis=1)
    both = lax.psum(dot32(part, base_both), "wide")
    columns = base_gate.shape[1]

    lefts = jnp.concatenate([gate_left, up_left], axis=0)
    low = lax.psum(jnp.einsum("td,edr->ter", rows, lefts, preferred_element_type=jnp.float32), "narrow")
    low = low.astype(bf16)

    mixed = 0.0
    thin = []
    for e in range(exp_here):
        gate = both[:, :columns] + dot32(low[:, e], gate_right[e])
        up = both[:, columns:] + dot32(low[:, exp_here + e], up_right[e])
        hidden = jax.nn.silu(gate) * up * weights[:, e : e + 1]
        mixed = mixed + hidden
        thin.append(dot32(hidden.astype(bf16), down_left[e]))
    mixed = lax.psum(mixed, "wide").astype(bf16)
    mixed_full = lax.all_gather(mixed, "narrow", axis=1, tiled=True)
    depth = base_down.shape[0]
    mixed_part = lax.dynamic_slice_in_dim(mixed_full, mine * depth, depth, axis=1)
    thin = lax.psum(jnp.concatenate(thin, axis=1), "narrow").astype(bf16)
    out = dot32(mixed_part, base_down) + dot32(thin, down_right.reshape(exp_here * rank, -1))
    out = lax.psum_scatter(out, "wide", scatter_dimension=0, tiled=True)
    return out.astype(bf16)


def solution(mesh):
    return jax.shard_map(
        shards,
        mesh=mesh,
        in_specs=(
            P(("groups", "wide"), "narrow"),
            P(("groups", "wide"), None),
            P(("groups", "wide"), None),
            P(),
            P("wide", "narrow"),
            P("wide", "narrow"),
            P("wide", "narrow"),
            P("wide", "narrow", None),
            P("wide", None, "narrow"),
            P("wide", "narrow", None),
            P("wide", None, "narrow"),
            P("wide", "narrow", None),
            P("wide", None, "narrow"),
        ),
        out_specs=P(("groups", "wide"), "narrow"),
        check_vma=False,
    )
```

```python
import jax
import jax.numpy as jnp
from jax import lax
from jax.experimental import pallas as pl
from jax.experimental.pallas import tpu as pltpu
from jax.sharding import PartitionSpec as P


def dot32(a, b):
    return jnp.dot(a, b, preferred_element_type=jnp.float32)


def dot32t(a, b):
    return lax.dot_general(a, b, (((1,), (1,)), ((), ())), preferred_element_type=jnp.float32)


PLANE = 4

LANES = 128


def kernel(
    tok, routes, shares, delta, bg_hbm, bu_hbm, bd_hbm, gl_hbm, gr, ul_hbm, ur, dl, dr_hbm, out,
    wt, bgu, lefts, bd, dr,
    xcol, xw, wts, gsend, grecv, gown, gred, gall, apart, asend, arecv, afin,
    hacc, hsend, hrecv, hpl, bpart, bsend, brecv, bfin, osend, orecv, oown,
    tok_s, tok_r, wt_s, wt_r, bs_s, bs_r, g_s, g_r, ga_s, ga_r, a_s, a_r,
    h_s, h_r, hb_s, hb_r, b_s, b_r, o_s, o_r, in_s,
):
    bf16, f32 = jnp.bfloat16, jnp.float32
    count = PLANE
    w, n = lax.axis_index("wide"), lax.axis_index("narrow")
    exp_here, rank, cols = gr.shape
    span = exp_here * rank
    loads = [
        pltpu.make_async_copy(gl_hbm, lefts.at[pl.ds(0, span)], in_s.at[0]),
        pltpu.make_async_copy(ul_hbm, lefts.at[pl.ds(span, span)], in_s.at[1]),
    ]
    chunk = LANES if cols % LANES == 0 else cols
    chunks = cols // chunk
    for c in range(chunks):
        for k, base in enumerate((bg_hbm, bu_hbm)):
            place = bgu.at[:, pl.ds((2 * c + k) * chunk, chunk)]
            loads.append(pltpu.make_async_copy(base.at[:, pl.ds(c * chunk, chunk)], place, in_s.at[2 + 2 * c + k]))
    loads.append(pltpu.make_async_copy(bd_hbm, bd, in_s.at[2 + 2 * chunks]))
    loads.append(pltpu.make_async_copy(dr_hbm, dr, in_s.at[3 + 2 * chunks]))
    for load in loads:
        load.start()
    pair = n + 1 - 2 * lax.rem(n, 2)
    across = lax.rem(n + 2, count)
    root = n == w
    relay = n == lax.rem(w + 2, count)

    def up_of(d):
        return lax.rem(w + d, count)

    def copy(src, dst, ss, rs, axis, peer):
        return pltpu.make_async_remote_copy(
            src_ref=src, dst_ref=dst, send_sem=ss, recv_sem=rs,
            device_id={axis: peer}, device_id_type=pl.DeviceIdType.MESH,
        )

    barrier = pltpu.get_barrier_semaphore()
    for d in range(1, count):
        pl.semaphore_signal(barrier, inc=1, device_id={"wide": up_of(d)}, device_id_type=pl.DeviceIdType.MESH)
    for peer in (pair, across):
        pl.semaphore_signal(barrier, inc=1, device_id={"narrow": peer}, device_id_type=pl.DeviceIdType.MESH)
    pl.semaphore_wait(barrier, count + 1)

    def tok_copy(d):
        return copy(tok, xcol.at[w], tok_s.at[d], tok_r.at[d], "wide", up_of(d))

    def wt_copy(d):
        return copy(wt, wts.at[w], wt_s.at[d], wt_r.at[d], "wide", up_of(d))

    def pair_copy(d, src):
        return copy(src, xw.at[up_of(count - d)], bs_s.at[d, 0], bs_r.at[d], "narrow", pair)

    def across_copy(d, src):
        return copy(src, xw.at[up_of(count - d)], bs_s.at[d, 1], bs_r.at[d], "narrow", across)

    for d in range(1, count):
        tok_copy(d).start()

    def g_copy(d, c, peer, slot):
        part = pl.ds(2 * c * chunk, 2 * chunk)
        return copy(gsend.at[peer, :, part], grecv.at[slot, :, part], g_s.at[d, c], g_r.at[d, c], "wide", peer)

    named, ids = routes[...], jnp.zeros(routes.shape, jnp.int32)
    for e in range(delta.shape[0]):
        ids = jnp.where(named == e, delta[e], ids)
    sets = lax.broadcasted_iota(jnp.int32, wt.shape, 0)
    table = jnp.zeros(sets.shape, f32)
    for k in range(routes.shape[0]):
        table = table + jnp.where(sets == ids[k : k + 1], shares[k : k + 1, :], 0.0)
    wt[...] = table
    for load in loads[:-2]:
        load.wait()

    def low(rows, b):
        apart[b] = dot32t(rows, lefts[...])

    for d in range(count):
        b = up_of(count - d)
        if d > 0:
            tok_copy(d).wait_recv()
        mine = tok if d == 0 else xcol.at[b]

        @pl.when(root)
        def _():
            across_copy(d, mine).start()
            pair_copy(d, mine).start()
            xw[b] = mine[...]

        low(mine[...], b)

        @pl.when(jnp.logical_not(root))
        def _():
            pair_copy(d, xw.at[b]).wait_recv()

        @pl.when(relay)
        def _():
            pair_copy(d, xw.at[b]).start()

        rows = xw[b]
        both = dot32(rows, bgu[...])
        if d == 0:
            gown[...] = both
            for k in range(1, count):
                wt_copy(k).start()
        else:
            gsend[b] = both.astype(bf16)
            for c in range(chunks):
                g_copy(d, c, b, w).start()

    def a_copy(k):
        return copy(asend.at[k], arecv.at[k], a_s.at[k], a_r.at[k], "narrow", (pair, across)[k])

    asend[0] = apart[...].astype(bf16)
    a_copy(0).start()
    a_copy(0).wait_recv()
    apart[...] = apart[...] + arecv[0].astype(f32)
    asend[1] = apart[...].astype(bf16)
    a_copy(1).start()

    def ga_copy(d, c):
        part = pl.ds(2 * c * chunk, 2 * chunk)
        return copy(gred.at[:, part], gall.at[w, :, part], ga_s.at[d, c], ga_r.at[d, c], "wide", up_of(d))

    for c in range(chunks):
        part = slice(2 * c * chunk, 2 * (c + 1) * chunk)
        total = gown[:, part]
        for d in range(1, count):
            g_copy(d, c, up_of(d), up_of(d)).wait_recv()
            total = total + grecv[up_of(d), :, part].astype(f32)
        gown[:, part] = total
        gred[:, part] = total.astype(bf16)
        for d in range(1, count):
            ga_copy(d, c).start()

    a_copy(1).wait_recv()
    afin[...] = (apart[...] + arecv[1].astype(f32)).astype(bf16)

    def h_copy(slot, c, target):
        part = pl.ds(c * chunk, chunk)
        return copy(hsend.at[:, :, part], hrecv.at[slot, :, :, part], h_s.at[c], h_r.at[slot, c], "wide", target)

    for c in range(chunks):
        gate_part = slice(2 * c * chunk, (2 * c + 1) * chunk)
        up_part = slice((2 * c + 1) * chunk, 2 * (c + 1) * chunk)
        part = slice(c * chunk, (c + 1) * chunk)
        for d in range(count):
            b = up_of(count - d)
            if d > 0:
                ga_copy(d, c).wait_recv()
                if c == 0:
                    wt_copy(d).wait_recv()
                gates, ups = gall[b, :, gate_part].astype(f32), gall[b, :, up_part].astype(f32)
                scales = wts[b].T
            else:
                gates, ups = gown[:, gate_part], gown[:, up_part]
                scales = wt[...].T
            ids = lax.broadcasted_iota(jnp.int32, scales.shape, 1)
            thin_rows = afin[b]
            acc = None
            for e in range(exp_here):
                scale = jnp.sum(jnp.where(ids == w * exp_here + e, scales, 0.0), axis=1, keepdims=True)
                own = slice(e * rank, (e + 1) * rank)
                gate = gates + dot32(thin_rows[:, own], gr[e, :, part])
                up = ups + dot32(thin_rows[:, span + e * rank : span + (e + 1) * rank], ur[e, :, part])
                hidden = gate / (1.0 + jnp.exp(-gate)) * up * scale
                acc = hidden if acc is None else acc + hidden
                thin = dot32t(hidden.astype(bf16), dl[e, :, part])
                bpart[b, :, own] = thin if c == 0 else bpart[b, :, own] + thin
            hacc[b, :, part] = acc
            hsend[b, :, part] = acc.astype(bf16)

        @pl.when(jnp.logical_not(root))
        def _():
            h_copy(w, c, n).start()

    def b_copy(k):
        return copy(bsend.at[k], brecv.at[k], b_s.at[k], b_r.at[k], "narrow", (pair, across)[k])

    bsend[0] = bpart[...].astype(bf16)
    b_copy(0).start()
    b_copy(0).wait_recv()
    bpart[...] = bpart[...] + brecv[0].astype(f32)
    bsend[1] = bpart[...].astype(bf16)
    b_copy(1).start()
    b_copy(1).wait_recv()
    bfin[...] = (bpart[...] + brecv[1].astype(f32)).astype(bf16)

    def hpair(d):
        b = up_of(count - d)
        return copy(hpl.at[b], hpl.at[b], hb_s.at[0, d], hb_r.at[d], "narrow", pair)

    def hacross(d):
        b = up_of(count - d)
        return copy(hpl.at[b], hpl.at[b], hb_s.at[1, d], hb_r.at[d], "narrow", across)

    for load in loads[-2:]:
        load.wait()

    for d in (2, 1, 3, 0):
        b = up_of(count - d)

        @pl.when(root)
        def _():
            whole = hacc[b]
            for k in range(1, count):
                src = up_of(k)
                if d == 2:
                    for c in range(chunks):
                        h_copy(src, c, src).wait_recv()
                whole = whole + hrecv[src, b].astype(f32)
            hpl[b] = whole.astype(bf16)
            hacross(d).start()
            hpair(d).start()

        @pl.when(jnp.logical_not(root))
        def _():
            hpair(d).wait_recv()

        @pl.when(relay)
        def _():
            hpair(d).start()

        part = dot32(hpl[b], bd[...]) + dot32(bfin[b], dr[...])
        if d == 0:
            oown[...] = part
        else:
            osend[b] = part.astype(bf16)
            copy(osend.at[b], orecv.at[w], o_s.at[d], o_r.at[d], "wide", b).start()
    total = oown[...]
    for d in (1, 3, 2):
        s = up_of(d)
        copy(osend.at[s], orecv.at[s], o_s.at[d], o_r.at[d], "wide", s).wait_recv()
        total = total + orecv[s].astype(f32)
    out[...] = total.astype(bf16)

    for d in range(1, count):
        b = up_of(count - d)
        tok_copy(d).wait_send()
        wt_copy(d).wait_send()
        for c in range(chunks):
            ga_copy(d, c).wait_send()
            g_copy(d, c, b, w).wait_send()
        copy(osend.at[b], orecv.at[w], o_s.at[d], o_r.at[d], "wide", b).wait_send()
    for k in range(2):
        a_copy(k).wait_send()
        b_copy(k).wait_send()

    @pl.when(root)
    def _():
        for d in range(count):
            src = tok if d == 0 else xcol.at[up_of(count - d)]
            across_copy(d, src).wait_send()
            pair_copy(d, src).wait_send()
            hacross(d).wait_send()
            hpair(d).wait_send()

    @pl.when(relay)
    def _():
        for d in range(count):
            pair_copy(d, xw.at[up_of(count - d)]).wait_send()
            hpair(d).wait_send()

    @pl.when(jnp.logical_not(root))
    def _():
        for c in range(chunks):
            h_copy(w, c, n).wait_send()


def fused(tokens, routes, shares, delta, bg, bu, bd, gl, gr, ul, ur, dl, dr):
    bf16, f32 = jnp.bfloat16, jnp.float32
    count = PLANE
    rows, feats = tokens.shape
    depth, cols = bg.shape
    exp_here, rank, _ = gr.shape
    span = exp_here * rank
    chunks = cols // LANES if cols % LANES == 0 else 1
    sem = pltpu.SemaphoreType.DMA
    vm = pltpu.VMEM
    out_feats = bd.shape[1]
    vmem, hbm = pl.BlockSpec(memory_space=pltpu.VMEM), pl.BlockSpec(memory_space=pl.ANY)
    return pl.pallas_call(
        kernel,
        out_shape=jax.ShapeDtypeStruct((rows, out_feats), bf16),
        in_specs=[
            vmem, vmem, vmem, pl.BlockSpec(memory_space=pltpu.SMEM),
            hbm, hbm, hbm, hbm, vmem, hbm, vmem, vmem, hbm,
        ],
        out_specs=pl.BlockSpec(memory_space=pltpu.VMEM),
        scratch_shapes=[
            vm((delta.shape[0], rows), f32),
            vm((depth, 2 * cols), bf16),
            vm((2 * span, feats), bf16),
            vm(bd.shape, bf16),
            vm((span, out_feats), bf16),
            vm((count, rows, feats), bf16),
            vm((count, rows, feats), bf16),
            vm((count, delta.shape[0], rows), f32),
            vm((count, rows, 2 * cols), bf16),
            vm((count, rows, 2 * cols), bf16),
            vm((rows, 2 * cols), f32),
            vm((rows, 2 * cols), bf16),
            vm((count, rows, 2 * cols), bf16),
            vm((count, rows, 2 * span), f32),
            vm((2, count, rows, 2 * span), bf16),
            vm((2, count, rows, 2 * span), bf16),
            vm((count, rows, 2 * span), bf16),
            vm((count, rows, cols), f32),
            vm((count, rows, cols), bf16),
            vm((count, count, rows, cols), bf16),
            vm((count, rows, cols), bf16),
            vm((count, rows, span), f32),
            vm((2, count, rows, span), bf16),
            vm((2, count, rows, span), bf16),
            vm((count, rows, span), bf16),
            vm((count, rows, out_feats), bf16),
            vm((count, rows, out_feats), bf16),
            vm((rows, out_feats), f32),
            sem((count,)), sem((count,)), sem((count,)), sem((count,)),
            sem((count, 2)), sem((count,)),
            sem((count, chunks)), sem((count, chunks)), sem((count, chunks)), sem((count, chunks)),
            sem((2,)), sem((2,)),
            sem((chunks,)), sem((count, chunks)), sem((2, count)), sem((count,)),
            sem((2,)), sem((2,)), sem((count,)), sem((count,)), sem((4 + 2 * chunks,)),
        ],
        compiler_params=pltpu.CompilerParams(collective_id=0, has_side_effects=True, vmem_limit_bytes=60 * 1024 * 1024),
    )(
        tokens, routes.T, shares.T, delta, bg, bu, bd,
        jnp.swapaxes(gl, 1, 2).reshape(span, feats), gr,
        jnp.swapaxes(ul, 1, 2).reshape(span, feats), ur,
        jnp.swapaxes(dl, 1, 2), dr.reshape(span, out_feats),
    )


def shards(
    tokens,
    routes,
    gate_weights,
    delta_of,
    base_gate,
    base_up,
    base_down,
    gate_left,
    gate_right,
    up_left,
    up_right,
    down_left,
    down_right,
):
    if lax.axis_size("narrow") == PLANE and lax.axis_size("wide") == PLANE:
        return fused(
            tokens, routes, gate_weights, delta_of, base_gate, base_up, base_down,
            gate_left, gate_right, up_left, up_right, down_left, down_right,
        )
    exp_here, _, rank = gate_left.shape
    experts = delta_of.shape[0]
    mine = lax.axis_index("wide")
    bf16 = jnp.bfloat16

    expert_ids = lax.broadcasted_iota(jnp.int32, (1, 1, experts), 2)
    named = routes[:, :, None] == expert_ids
    delta_ids = jnp.sum(jnp.where(named, delta_of[None, None, :], 0), axis=2)
    weight_of = jnp.sum(
        jnp.where(delta_ids[:, :, None] == expert_ids, gate_weights[:, :, None], 0.0), axis=1
    )
    weights = lax.all_gather(weight_of, "wide", axis=0, tiled=True)
    weights = lax.dynamic_slice_in_dim(weights, mine * exp_here, exp_here, axis=1)

    rows = lax.all_gather(tokens, "wide", axis=0, tiled=True)
    full = lax.all_gather(rows, "narrow", axis=1, tiled=True)
    depth = base_gate.shape[0]
    part = lax.dynamic_slice_in_dim(full, mine * depth, depth, axis=1)

    base_both = jnp.concatenate([base_gate, base_up], axis=1)
    both = lax.psum(dot32(part, base_both), "wide")
    columns = base_gate.shape[1]

    lefts = jnp.concatenate([gate_left, up_left], axis=0)
    low = lax.psum(jnp.einsum("td,edr->ter", rows, lefts, preferred_element_type=jnp.float32), "narrow")
    low = low.astype(bf16)

    mixed = 0.0
    thin = []
    for e in range(exp_here):
        gate = both[:, :columns] + dot32(low[:, e], gate_right[e])
        up = both[:, columns:] + dot32(low[:, exp_here + e], up_right[e])
        hidden = jax.nn.silu(gate) * up * weights[:, e : e + 1]
        mixed = mixed + hidden
        thin.append(dot32(hidden.astype(bf16), down_left[e]))
    mixed = lax.psum(mixed, "wide").astype(bf16)
    mixed_full = lax.all_gather(mixed, "narrow", axis=1, tiled=True)
    depth = base_down.shape[0]
    mixed_part = lax.dynamic_slice_in_dim(mixed_full, mine * depth, depth, axis=1)
    thin = lax.psum(jnp.concatenate(thin, axis=1), "narrow").astype(bf16)
    out = dot32(mixed_part, base_down) + dot32(thin, down_right.reshape(exp_here * rank, -1))
    out = lax.psum_scatter(out, "wide", scatter_dimension=0, tiled=True)
    return out.astype(bf16)


def solution(mesh):
    return jax.shard_map(
        shards,
        mesh=mesh,
        in_specs=(
            P(("groups", "wide"), "narrow"),
            P(("groups", "wide"), None),
            P(("groups", "wide"), None),
            P(),
            P("wide", "narrow"),
            P("wide", "narrow"),
            P("wide", "narrow"),
            P("wide", "narrow", None),
            P("wide", None, "narrow"),
            P("wide", "narrow", None),
            P("wide", None, "narrow"),
            P("wide", "narrow", None),
            P("wide", None, "narrow"),
        ),
        out_specs=P(("groups", "wide"), "narrow"),
        check_vma=False,
    )
```
